128 devices in a mesh: freq: 8 (over z, x_hi), rcv: 16 (over x_lo, y, core).
Axes of the slice: x: 4 (x_hi: 2, x_lo: 2; x = x_hi * 2 + x_lo), y: 4, z: 4, core: 2. Of those that a mesh axis runs over, the one named last changes fastest.
Arguments:
- reflection: float32 [128, 2, 1024, 2048], P('freq', None, None, 'rcv'), may hold values from -0.09375 to 0.09375
- focusing_input: float32 [128, 2, 32, 2048], P('freq', None, None, 'rcv'), may hold values from -6 to 6
- direct_wave: float32 [256, 32, 2048], P(None, 'freq', 'rcv'), may hold values from -6 to 6
- mute_source: int32 [32, 1024], P('rcv', 'freq'), may hold values from 32 to 127
- mute_receiver: int32 [32, 2048], P('freq', 'rcv'), may hold values from 32 to 127
Outputs:
- focus_minus: float32 [256, 32, 1024], P(None, 'rcv', 'freq')
- focus_plus: float32 [256, 32, 2048], P(None, 'freq', 'rcv')
The draws below stay inside these ranges and needn't reach their ends.
All inputs are finite; a program needn't handle non-finite values.
Results may differ from the reference program's by a relative error of at most 0.00007.
Values sent between devices are 32-bit elements; how exact they have to be, the bound alone decides.
No kernel may reach another device: no remote copies, remote signals or barrier semaphores. Data moves between devices by JAX's collectives and lax.ppermute only.
A program may use at most 128 MiB of HBM per device.

```python
import math
import jax
import jax.numpy as jnp
from jax import lax

F = 128
S = 1024
RCV = 2048
P_SIZE = 32
NT = 256


def set_ends(array, rng, least, top_value):
    longest = array.shape.index(max(array.shape))
    spots = []
    for shift in (0, 1):
        where = [jax.random.randint(jax.random.fold_in(rng, axis), (), 0, length) for axis, length in enumerate(array.shape)]
        where[longest] = (where[longest] + shift) % array.shape[longest]
        spots.append(tuple(where))
    return array.at[spots[0]].set(least).at[spots[1]].set(top_value)


def block_scale(own_key, shape, pieces, smallest, top_value):
    gain, own = 1.0, jax.random.fold_in(own_key, 6)
    for position, blocks in pieces:
        heights = jnp.exp(jax.random.uniform(jax.random.fold_in(own, position), (blocks,), jnp.float32, smallest / len(pieces), top_value / len(pieces)))
        gain = gain * jnp.repeat(heights, shape[position] // blocks).reshape([-1 if axis == position else 1 for axis in range(len(shape))])
    return gain


def gaussian(key, dims, width, limit, cuts=(), kind=jnp.bfloat16):
    loudness = block_scale(key, dims, cuts, -0.22, 0.18) if cuts else 1.0
    values = jax.random.normal(key, dims, jnp.float32) * width * loudness
    return jnp.minimum(jnp.maximum(values, -limit), limit).astype(kind)


def setup_inputs(seed: int = 0) -> dict:
    key_of = jax.random.split(jax.random.key(seed), 6)
    reflection = gaussian(key_of[0], (F, 2, S, RCV), (2 * RCV) ** -0.5, 0.09375, ((0, 8), (3, 16)), jnp.float32)
    focusing_input = gaussian(key_of[1], (F, 2, P_SIZE, RCV), 1.0, 6.0, ((0, 8), (3, 16)), jnp.float32)
    direct_wave = gaussian(key_of[2], (NT, P_SIZE, RCV), 1.0, 6.0, ((1, 8), (2, 16)), jnp.float32)
    mute_source = set_ends(jax.random.randint(key_of[3], (P_SIZE, S), NT // 8, NT // 2), jax.random.fold_in(key_of[3], 1), NT // 8, (NT // 2) - 1).astype(jnp.int32)
    mute_receiver = set_ends(jax.random.randint(key_of[4], (P_SIZE, RCV), NT // 8, NT // 2), jax.random.fold_in(key_of[4], 1), NT // 8, (NT // 2) - 1).astype(jnp.int32)
    return dict(reflection=reflection, focusing_input=focusing_input, direct_wave=direct_wave, mute_source=mute_source, mute_receiver=mute_receiver)


MAXIMUM_ACCURACY = lax.Precision.HIGHEST

def dft_tables():
    index_freq = jnp.arange(F, dtype=jnp.int32)[:, None] + 1
    index_time = jnp.arange(NT, dtype=jnp.int32)[None, :]
    phase_turns = jnp.mod(index_freq * index_time, NT).astype(jnp.float32) * (2.0 * math.pi / NT)
    return (jnp.cos(phase_turns), jnp.sin(phase_turns))

def window(traces, mute_table):
    time_index = jnp.arange(NT, dtype=jnp.int32)[:, None, None]
    kept_mask = (time_index < mute_table[None]) | (time_index > NT - mute_table[None])
    return jnp.where(kept_mask, traces, jnp.zeros_like(traces))

def reference(reflection, focusing_input, direct_wave, mute_source, mute_receiver):
    cosine, sine_table = dft_tables()
    factor = 1.0 / math.sqrt(F)
    reflection_real = reflection[:, 0]
    reflection_imaginary = reflection[:, 1]
    focusing_real = focusing_input[:, 0]
    focusing_imaginary = focusing_input[:, 1]
    upgoing_real = jnp.einsum('ual,uel->eua', reflection_real, focusing_real, precision=MAXIMUM_ACCURACY) - jnp.einsum('ual,uel->eua', reflection_imaginary, focusing_imaginary, precision=MAXIMUM_ACCURACY)
    upgoing_imaginary = jnp.einsum('ual,uel->eua', reflection_real, focusing_imaginary, precision=MAXIMUM_ACCURACY) + jnp.einsum('ual,uel->eua', reflection_imaginary, focusing_real, precision=MAXIMUM_ACCURACY)
    up_time = factor * (jnp.einsum('pfs,ft->tps', upgoing_real, cosine, precision=MAXIMUM_ACCURACY) - jnp.einsum('pfs,ft->tps', upgoing_imaginary, sine_table, precision=MAXIMUM_ACCURACY))
    focus_minus = window(up_time, mute_source)
    backward_real = factor * jnp.einsum('tps,ft->pfs', focus_minus, cosine, precision=MAXIMUM_ACCURACY)
    backward_imaginary = -factor * jnp.einsum('tps,ft->pfs', focus_minus, sine_table, precision=MAXIMUM_ACCURACY)
    adjoint_real_values = jnp.einsum('klh,lhc->klc', backward_real, reflection_real, precision=MAXIMUM_ACCURACY) + jnp.einsum('klh,lhc->klc', backward_imaginary, reflection_imaginary, precision=MAXIMUM_ACCURACY)
    adjoint_imaginary = jnp.einsum('klh,lhc->klc', backward_imaginary, reflection_real, precision=MAXIMUM_ACCURACY) - jnp.einsum('klh,lhc->klc', backward_real, reflection_imaginary, precision=MAXIMUM_ACCURACY)
    adj_time = factor * (jnp.einsum('pfr,ft->tpr', adjoint_real_values, cosine, precision=MAXIMUM_ACCURACY) - jnp.einsum('pfr,ft->tpr', adjoint_imaginary, sine_table, precision=MAXIMUM_ACCURACY))
    focus_plus = direct_wave - window(adj_time, mute_receiver)
    return (focus_minus, focus_plus)
```

```python
import math

import numpy as np
import jax
import jax.numpy as jnp
from jax import lax
from jax.experimental import pallas as pl
from jax.experimental.pallas import tpu as pltpu
from jax.sharding import Mesh, PartitionSpec as P

F32, BF16 = jnp.float32, jnp.bfloat16
NT = 256
KB, KK = 8, 16


def dft_table():
    k = np.arange(1, KB * KK + 1)[None, :]
    t = np.arange(NT)[:, None]
    phase = 2.0 * math.pi * ((k * t) % NT) / NT
    c = 1.0 / math.sqrt(KB * KK)
    both = np.stack([c * np.cos(phase), -c * np.sin(phase)], axis=1)
    return both.reshape(NT, 2, KB, KK).transpose(0, 2, 1, 3).reshape(NT, NT)


def split_const(table):
    high = table.astype(np.float32).astype(jnp.bfloat16)
    low = (table - high.astype(np.float64)).astype(np.float32).astype(jnp.bfloat16)
    return np.asarray(high), np.asarray(low)


def split(x):
    high = x.astype(BF16)
    return high, (x - high.astype(F32)).astype(BF16)


def mm(a, b, contract=(1, 0)):
    return lax.dot_general(a, b, (((contract[0],), (contract[1],)), ((), ())), preferred_element_type=F32)


def mm3(a, b):
    return mm(a[0], b[0]) + (mm(a[0], b[1]) + mm(a[1], b[0]))


def forward_kernel(perm_ref, f_ref, r_ref, own_ref, oth_ref):
    perm = perm_ref[...]
    for q in range(2):
        fr, fi = f_ref[q, 0], f_ref[q, 1]
        x = jnp.concatenate(
            [jnp.concatenate([fr, -fi], axis=1), jnp.concatenate([fi, fr], axis=1)], axis=0
        )
        xh, xl = split(x)
        ph, plo = mm(perm, xh).astype(BF16), mm(perm, xl).astype(BF16)
        lhs = jnp.concatenate([ph, plo], axis=0)
        for z in range(4):
            rows = slice(z * 256, (z + 1) * 256)
            w = jnp.concatenate([r_ref[q, 0, rows, :], r_ref[q, 1, rows, :]], axis=1)
            wh, wl = split(w)
            acc = mm(lhs, wh, (1, 1))
            res = acc[:64] + (acc[64:] + mm(ph, wl, (1, 1)))
            res = res.reshape(2, 8, 4, 256)
            for xh_ in range(2):
                part = res[:, :, :, xh_ * 128 : (xh_ + 1) * 128]
                own_ref[xh_ * 8 : (xh_ + 1) * 8, z, q * 4 : (q + 1) * 4, :] = part[0]
                oth_ref[xh_ * 8 : (xh_ + 1) * 8, z, q * 4 : (q + 1) * 4, :] = part[1]


def forward_panel(reflection, focusing, perm):
    panel = jax.ShapeDtypeStruct((16, 4, 64, 128), F32)
    spec = pl.BlockSpec((16, 4, 8, 128), lambda i: (0, 0, i, 0))
    return pl.pallas_call(
        forward_kernel,
        grid=(8,),
        in_specs=[
            pl.BlockSpec((64, 64), lambda i: (0, 0)),
            pl.BlockSpec((2, 2, 32, 128), lambda i: (i, 0, 0, 0)),
            pl.BlockSpec((2, 2, 1024, 128), lambda i: (i, 0, 0, 0)),
        ],
        out_specs=[spec, spec],
        out_shape=[panel, panel],
        compiler_params=pltpu.CompilerParams(vmem_limit_bytes=40 * 2**20),
        cost_estimate=pl.CostEstimate(flops=3 * 2**30, bytes_accessed=21 * 2**20, transcendentals=0),
        name="forward_panel",
    )(perm, focusing, reflection)


def source_kernel(th_ref, tl_ref, tth_ref, ttl_ref, mute_ref, x_ref, time_ref, spec_ref):
    cols = []
    for j in range(2):
        pieces = [
            x_ref[kb, pl.ds(ri * 2 + j, KK, stride=4), :] for kb in range(KB) for ri in range(2)
        ]
        cols.append(jnp.concatenate(pieces, axis=0))
    u = split(jnp.concatenate(cols, axis=1))
    up = mm3((th_ref[...], tl_ref[...]), u)
    t = lax.broadcasted_iota(jnp.int32, (NT, 128), 0)
    kept = []
    for j in range(2):
        mute = jnp.broadcast_to(mute_ref[j : j + 1, :], (NT, 128))
        val = jnp.where((t < mute) | (t > NT - mute), up[:, j * 128 : (j + 1) * 128], 0.0)
        time_ref[pl.ds(j, NT, stride=2), :] = val
        kept.append(val)
    w = split(jnp.concatenate(kept, axis=1))
    back = mm3((tth_ref[...], ttl_ref[...]), w)
    for j in range(2):
        for kb in range(KB):
            for ri in range(2):
                row = kb * 32 + ri * 16
                spec_ref[kb, pl.ds(ri * 2 + j, KK, stride=4), :] = back[
                    row : row + 16, j * 128 : (j + 1) * 128
                ]


def source_traces(tables, mute, x):
    return pl.pallas_call(
        source_kernel,
        out_shape=[
            jax.ShapeDtypeStruct((NT * 2, 128), F32),
            jax.ShapeDtypeStruct((KB, 64, 128), F32),
        ],
        compiler_params=pltpu.CompilerParams(vmem_limit_bytes=40 * 2**20),
        name="source_traces",
    )(*tables, mute, x)


def adjoint_kernel(own_ref, oth_ref, r_ref, out_ref):
    sub = lax.broadcasted_iota(jnp.int32, (64, 128), 0)
    lower = (sub % 8) < 4
    first = (sub % 4) < 2

    def swap4(v):
        return jnp.where(lower, pltpu.roll(v, 60, 0), pltpu.roll(v, 4, 0))

    acc = [None, None]
    for z in range(4):
        lhs = [[], []]
        for xh_ in range(2):
            own = own_ref[xh_ * 8 : (xh_ + 1) * 8, z, :, :].reshape(64, 128)
            oth = oth_ref[xh_ * 8 : (xh_ + 1) * 8, z, :, :].reshape(64, 128)
            lhs[0].append(jnp.where(lower, own, swap4(oth)))
            lhs[1].append(jnp.where(lower, swap4(own), oth))
        for q in range(2):
            bh, bl = split(jnp.concatenate(lhs[q], axis=1))
            rows = slice(z * 256, (z + 1) * 256)
            wh, wl = split(jnp.concatenate([r_ref[q, 0, rows, :], r_ref[q, 1, rows, :]], axis=1))
            both = mm(jnp.concatenate([bh, bl], axis=0), wh)
            add = both[:64] + (both[64:] + mm(bh, wl))
            acc[q] = add if acc[q] is None else acc[q] + add
    for q in range(2):
        p_, q_ = acc[q][:, :128], acc[q][:, 128:]
        res = p_ + jnp.where(first, pltpu.roll(q_, 62, 0), -pltpu.roll(q_, 2, 0))
        out_ref[:, q * 8 : (q + 1) * 8, :] = res.reshape(8, 8, 128)


def adjoint_panel(own, oth, reflection):
    spec = pl.BlockSpec((16, 4, 8, 128), lambda i: (0, 0, i, 0))
    return pl.pallas_call(
        adjoint_kernel,
        grid=(8,),
        in_specs=[spec, spec, pl.BlockSpec((2, 2, 1024, 128), lambda i: (i, 0, 0, 0))],
        out_specs=pl.BlockSpec((8, 16, 128), lambda i: (0, i, 0)),
        out_shape=jax.ShapeDtypeStruct((8, 128, 128), F32),
        compiler_params=pltpu.CompilerParams(vmem_limit_bytes=40 * 2**20),
        cost_estimate=pl.CostEstimate(flops=3 * 2**30, bytes_accessed=21 * 2**20, transcendentals=0),
        name="adjoint_panel",
    )(own, oth, reflection)


def receiver_kernel(core_ref, th_ref, tl_ref, mute_ref, direct_ref, x_ref, out_ref):
    even = core_ref[0] == 0
    t = lax.broadcasted_iota(jnp.int32, (NT, 128), 0)
    for c in range(2):
        cols = []
        for j in range(2):
            pieces = []
            for kb in range(KB):
                for ri in range(2):
                    a = x_ref[kb, pl.ds(c * 4 + ri * 2 + j, KK, stride=8), :]
                    b = x_ref[kb, pl.ds((1 - c) * 4 + ri * 2 + j, KK, stride=8), :]
                    pieces.append(jnp.where(even, a, b))
            cols.append(jnp.concatenate(pieces, axis=0))
        adj = mm3((th_ref[...], tl_ref[...]), split(jnp.concatenate(cols, axis=1)))
        for j in range(2):
            p = c * 2 + j
            mute = jnp.broadcast_to(mute_ref[p : p + 1, :], (NT, 128))
            val = jnp.where((t < mute) | (t > NT - mute), adj[:, j * 128 : (j + 1) * 128], 0.0)
            rows = pl.ds(p, NT, stride=4)
            out_ref[rows, :] = direct_ref[rows, :] - val


def receiver_traces(core, tables, mute, direct, x):
    vmem = pl.BlockSpec(memory_space=pltpu.VMEM)
    return pl.pallas_call(
        receiver_kernel,
        in_specs=[pl.BlockSpec(memory_space=pltpu.SMEM)] + [vmem] * 5,
        out_specs=vmem,
        out_shape=jax.ShapeDtypeStruct((NT * 4, 128), F32),
        compiler_params=pltpu.CompilerParams(vmem_limit_bytes=40 * 2**20),
        name="receiver_traces",
    )(core, *tables, mute, direct, x)


def body(reflection, focusing, direct_wave, mute_source, mute_receiver):
    core = lax.axis_index("c")
    table = dft_table()
    th, tl = split_const(table)
    row = lax.broadcasted_iota(jnp.int32, (64, 64), 0)
    col = lax.broadcasted_iota(jnp.int32, (64, 64), 1)
    crel, dev, ri, j = row // 32, (row // 4) % 8, (row // 2) % 2, row % 2
    perm = (col == ri * 32 + dev * 4 + ((crel + core) % 2) * 2 + j).astype(BF16)

    swap = [(0, 1), (1, 0)]
    around = ("xh", "xl", "y")
    own, oth = forward_panel(reflection, focusing, perm)
    panel = own + lax.ppermute(oth, "c", swap)
    parts = lax.all_to_all(panel, around, split_axis=0, concat_axis=0, tiled=True)
    summed = jnp.sum(parts.reshape(2, 8, 4, 64, 128), axis=1).transpose(1, 0, 2, 3)
    spectrum = lax.all_to_all(summed, "z", split_axis=0, concat_axis=0, tiled=True)
    time, back = source_traces((th, tl, th.T, tl.T), mute_source, spectrum.reshape(8, 64, 128))
    back = lax.all_to_all(back.reshape(4, 2, 64, 128), "z", split_axis=0, concat_axis=0, tiled=True)
    wide = jnp.broadcast_to(back.transpose(1, 0, 2, 3)[:, None], (2, 8, 4, 64, 128))
    b_own = lax.all_to_all(wide.reshape(16, 4, 64, 128), around, split_axis=0, concat_axis=0, tiled=True)
    b_oth = lax.ppermute(b_own, "c", swap)
    adjoint = adjoint_panel(b_own, b_oth, reflection)
    received = lax.all_to_all(adjoint, ("z", "xh"), split_axis=0, concat_axis=0, tiled=True)
    plus = receiver_traces(
        core.reshape(1), (th, tl), mute_receiver, direct_wave.reshape(NT * 4, 128), received
    )
    return time.reshape(NT, 2, 128), plus.reshape(NT, 4, 128)


def solution(mesh):
    fine = Mesh(mesh.devices.reshape(4, 2, 2, 4, 2), ("z", "xh", "xl", "y", "c"))
    freq, rcv = ("z", "xh"), ("xl", "y", "c")
    return jax.shard_map(
        body,
        mesh=fine,
        in_specs=(
            P(freq, None, None, rcv),
            P(freq, None, None, rcv),
            P(None, freq, rcv),
            P(rcv, freq),
            P(freq, rcv),
        ),
        out_specs=(P(None, rcv, freq), P(None, freq, rcv)),
        check_vma=False,
    )
```

```python
import functools
import math

import numpy as np
import jax
import jax.numpy as jnp
from jax import lax
from jax.experimental import pallas as pl
from jax.experimental.pallas import tpu as pltpu
from jax.sharding import Mesh, PartitionSpec as P

F32, BF16 = jnp.float32, jnp.bfloat16
NT = 256
KB, KK = 8, 16
VMEM = pl.BlockSpec(memory_space=pltpu.VMEM)
SMEM = pl.BlockSpec(memory_space=pltpu.SMEM)
HBM = pl.BlockSpec(memory_space=pltpu.HBM)


def dft_table():
    k = np.arange(1, KB * KK + 1)[None, :]
    t = np.arange(NT)[:, None]
    phase = 2.0 * math.pi * ((k * t) % NT) / NT
    c = 1.0 / math.sqrt(KB * KK)
    return np.stack([c * np.cos(phase), -c * np.sin(phase)], axis=2).reshape(NT, NT)


def split_const(table):
    high = table.astype(np.float32).astype(jnp.bfloat16)
    low = (table - high.astype(np.float64)).astype(np.float32).astype(jnp.bfloat16)
    return np.asarray(high), np.asarray(low)


def split(x):
    high = x.astype(BF16)
    return high, (x - high.astype(F32)).astype(BF16)


def mm(a, b, contract=(1, 0)):
    return lax.dot_general(a, b, (((contract[0],), (contract[1],)), ((), ())), preferred_element_type=F32)


def mm3(a, b):
    return mm(a[0], b[0]) + (mm(a[0], b[1]) + mm(a[1], b[0]))


def params(mib):
    return pltpu.CompilerParams(vmem_limit_bytes=mib * 2**20)


def trade(v, pair, shift):
    t = v[(0 - shift) % 4]
    for m in range(1, 4):
        t = jnp.where(pair == m, v[(m - shift) % 4], t)
    return t


def unturn(x, y, sign):
    out = x
    for s in range(1, 4):
        out = jnp.where(y == s, pltpu.roll(x, (sign * 2 * s) % 8, 1), out)
    return out


def fetch_piece(r_hbm, r_ref, sem, g, z):
    cut = (pl.ds(g * 4, 4), slice(None), pl.ds(z * 256, 256))
    return pltpu.make_async_copy(r_hbm.at[cut], r_ref.at[cut], sem.at[g * 4 + z])


def forward_kernel(core_ref, f_hbm, r_hbm, own0, own1, oth0, oth1, f_ref, r_ref, fsem, sem):
    outs = (own0, own1, oth0, oth1)

    fetch = functools.partial(fetch_piece, r_hbm, r_ref, sem)
    fcopy = pltpu.make_async_copy(f_hbm, f_ref, fsem)
    fcopy.start()
    for g in range(4):
        for z in range(4):
            fetch(g, z).start()
    core = core_ref[0]
    row = lax.broadcasted_iota(jnp.int32, (64, 64), 0)
    col = lax.broadcasted_iota(jnp.int32, (64, 64), 1)
    perms = []
    for q in range(4):
        c = (row // 32 + core) % 2
        y = ((row // 2) % 4 + 4 - q) % 4
        src = (row % 2) * 32 + ((row // 8) % 2) * 16 + y * 4 + c * 2 + (row // 16) % 2
        perms.append(jnp.where(col == src, 1.0, 0.0).astype(BF16))
    pair = lax.broadcasted_iota(jnp.int32, (8, 128), 0) // 2
    fcopy.wait()

    @pl.loop(0, 4)
    def _(g):
        lhs = []
        for q in range(4):
            fr, fi = f_ref[g * 4 + q, 0], f_ref[g * 4 + q, 1]
            x = jnp.concatenate(
                [jnp.concatenate([fr, -fi], axis=1), jnp.concatenate([fi, fr], axis=1)], axis=0
            )
            xh, xl = split(x)
            ph, plo = mm(perms[q], xh).astype(BF16), mm(perms[q], xl).astype(BF16)
            lhs.append((ph, jnp.concatenate([ph, plo], axis=0)))
        g8 = pl.ds(pl.multiple_of(g * 8, 8), 8)
        for z in range(4):
            fetch(g, z).wait()
            rows = slice(z * 256, (z + 1) * 256)
            res = []
            for q in range(4):
                k = g * 4 + q
                wh, wl = split(jnp.concatenate([r_ref[k, 0, rows, :], r_ref[k, 1, rows, :]], axis=1))
                acc = mm(lhs[q][1], wh, (1, 1))
                res.append(acc[:64] + (acc[64:] + mm(lhs[q][0], wl, (1, 1))))
            for xh_ in range(2):
                for part in range(8):
                    v = [r[part * 8 : part * 8 + 8, xh_ * 128 : xh_ * 128 + 128] for r in res]
                    out, xlo = outs[part // 2], part % 2
                    for y in range(4):
                        out[xh_ * 8 + xlo * 4 + y, z, g8, :] = trade(v, pair, y)


def forward_panel(core, focusing, reflection):
    panel = jax.ShapeDtypeStruct((16, 4, 32, 128), F32)
    return pl.pallas_call(
        forward_kernel,
        in_specs=[SMEM, HBM, HBM],
        out_specs=[VMEM] * 4,
        out_shape=[panel] * 4,
        scratch_shapes=[
            pltpu.VMEM((KK, 2, 32, 128), F32),
            pltpu.VMEM((KK, 2, 1024, 128), F32),
            pltpu.SemaphoreType.DMA,
            pltpu.SemaphoreType.DMA((16,)),
        ],
        compiler_params=params(24),
        cost_estimate=pl.CostEstimate(flops=3 * 2**30, bytes_accessed=21 * 2**20, transcendentals=0),
        name="forward_panel",
    )(core, focusing, reflection)


def sum_kernel(pos_ref, x_ref, o0, o1, o2, o3):
    z = pos_ref[0]
    for d, out in enumerate((o0, o1, o2, o3)):
        zz = lax.rem(z + d, 4)
        for h in range(2):
            t = [x_ref[h * 8 + i, zz] for i in range(8)]
            out[h] = ((t[0] + t[1]) + (t[2] + t[3])) + ((t[4] + t[5]) + (t[6] + t[7]))


def sum_parts(pos, parts):
    piece = jax.ShapeDtypeStruct((2, 32, 128), F32)
    return pl.pallas_call(
        sum_kernel,
        in_specs=[SMEM, VMEM],
        out_specs=[VMEM] * 4,
        out_shape=[piece] * 4,
        compiler_params=params(4),
        name="sum_parts",
    )(pos, parts)


def source_kernel(j, pos_ref, th_ref, tl_ref, tth_ref, ttl_ref, mute_ref, x0, x1, x2, x3, *rest):
    time_ref, b0, b1, b2, b3, tmp = rest[-6:]
    z, y = pos_ref[0], pos_ref[1]
    for d, x in enumerate((x0, x1, x2, x3)):
        src = lax.rem(z + 4 - d, 4)
        tmp[src] = unturn(x[...].reshape(8, 8, 128), y, -1).reshape(2, 32, 128)
    up = mm3((th_ref[...], tl_ref[...]), split(tmp[...].reshape(256, 128)))
    t = lax.broadcasted_iota(jnp.int32, (NT, 128), 0)
    mute = jnp.broadcast_to(mute_ref[j : j + 1, :], (NT, 128))
    val = jnp.where((t < mute) | (t > NT - mute), up, 0.0)
    time_ref[pl.ds(j, NT, stride=2), :] = val
    if j == 1:
        time_ref[pl.ds(0, NT, stride=2), :] = rest[0][...]
    back = mm3((tth_ref[...], ttl_ref[...]), split(val))
    tmp[...] = unturn(back.reshape(32, 8, 128), y, 1).reshape(4, 2, 32, 128)
    for d, out in enumerate((b0, b1, b2, b3)):
        out[...] = tmp[lax.rem(z + d, 4)]


def source_traces(j, pos, tables, mute, pieces, first):
    piece = jax.ShapeDtypeStruct((2, 32, 128), F32)
    time = jax.ShapeDtypeStruct((NT * 2, 128), F32)
    if j == 0:
        kernel, extra, shape = functools.partial(source_first, source_kernel), (), (NT, 128)
        time = jax.ShapeDtypeStruct(shape, F32)
    else:
        kernel, extra = functools.partial(source_kernel, 1), (first,)
    return pl.pallas_call(
        kernel,
        in_specs=[SMEM] + [VMEM] * (9 + len(extra)),
        out_specs=[VMEM] * 5,
        out_shape=[time] + [piece] * 4,
        scratch_shapes=[pltpu.VMEM((4, 2, 32, 128), F32)],
        compiler_params=params(8),
        name=f"source_traces{j}",
    )(pos, *tables, mute, *pieces, *extra)


class _Rows:
    def __init__(self, ref):
        self.ref = ref

    def __setitem__(self, index, value):
        self.ref[...] = value


def source_first(kernel, *refs):
    refs = list(refs)
    refs[-6] = _Rows(refs[-6])
    kernel(0, *refs)


def spread_kernel(pos_ref, x0, x1, x2, x3, out_ref):
    z = pos_ref[0]
    for d, x in enumerate((x0, x1, x2, x3)):
        src = lax.rem(z + 4 - d, 4)
        for h in range(2):
            val = x[h]
            for i in range(8):
                out_ref[h * 8 + i, src] = val


def spread(pos, pieces):
    return pl.pallas_call(
        spread_kernel,
        in_specs=[SMEM] + [VMEM] * 4,
        out_specs=VMEM,
        out_shape=jax.ShapeDtypeStruct((16, 4, 32, 128), F32),
        compiler_params=params(4),
        name="spread",
    )(pos, *pieces)


def adjoint_kernel(o0, o1, t0, t1, r_hbm, out_ref, r_ref, sem):
    fetch = functools.partial(fetch_piece, r_hbm, r_ref, sem)
    for g in range(4):
        for z in range(4):
            fetch(g, z).start()
    pair = lax.broadcasted_iota(jnp.int32, (8, 128), 0) // 2
    even = (lax.broadcasted_iota(jnp.int32, (64, 128), 0) % 2) == 0

    @pl.loop(0, 4)
    def _(g):
        g8 = pl.ds(pl.multiple_of(g * 8, 8), 8)
        acc = [None] * 4
        for z in range(4):
            lhs = [[None] * 2 for _ in range(4)]
            for xh_ in range(2):
                tiles = [[] for _ in range(4)]
                for ref in (o0, t0, o1, t1):
                    for xlo in range(2):
                        v = [ref[xh_ * 8 + xlo * 4 + y, z, g8, :] for y in range(4)]
                        for q in range(4):
                            tiles[q].append(trade(v, pair, q))
                for q in range(4):
                    lhs[q][xh_] = jnp.concatenate(tiles[q], axis=0)
            rows = slice(z * 256, (z + 1) * 256)
            fetch(g, z).wait()
            for q in range(4):
                k = g * 4 + q
                bh, bl = split(jnp.concatenate(lhs[q], axis=1))
                wh, wl = split(jnp.concatenate([r_ref[k, 0, rows, :], r_ref[k, 1, rows, :]], axis=1))
                both = mm(jnp.concatenate([bh, bl], axis=0), wh)
                add = both[:64] + (both[64:] + mm(bh, wl))
                acc[q] = add if acc[q] is None else acc[q] + add
        res = []
        for q in range(4):
            a, b = acc[q][:, :128], acc[q][:, 128:]
            res.append(a + jnp.where(even, pltpu.roll(b, 63, 0), -pltpu.roll(b, 1, 0)))
        for part in range(8):
            v = [r[part * 8 : part * 8 + 8] for r in res]
            for y in range(4):
                out_ref[(part % 2) * 4 + y, part // 2, g8, :] = trade(v, pair, y)


def adjoint_panel(own, oth, reflection):
    return pl.pallas_call(
        adjoint_kernel,
        in_specs=[VMEM] * 4 + [HBM],
        out_specs=VMEM,
        out_shape=jax.ShapeDtypeStruct((8, 4, 32, 128), F32),
        scratch_shapes=[pltpu.VMEM((KK, 2, 1024, 128), F32), pltpu.SemaphoreType.DMA((16,))],
        compiler_params=params(24),
        cost_estimate=pl.CostEstimate(flops=3 * 2**30, bytes_accessed=21 * 2**20, transcendentals=0),
        name="adjoint_panel",
    )(*own, *oth, reflection)


def receiver_kernel(pos_ref, th_ref, tl_ref, mute_ref, direct_ref, x_ref, out_ref):
    even = pos_ref[2] == 0
    turn = pos_ref[3]
    t = lax.broadcasted_iota(jnp.int32, (NT, 128), 0)
    for c in range(2):
        cols = []
        for j in range(2):
            a = jnp.where(even, x_ref[:, j * 2 + c], x_ref[:, j * 2 + 1 - c])
            cols.append(unturn(a.reshape(32, 8, 128), turn, -1).reshape(256, 128))
        adj = mm3((th_ref[...], tl_ref[...]), split(jnp.concatenate(cols, axis=1)))
        for j in range(2):
            p = c * 2 + j
            mute = jnp.broadcast_to(mute_ref[p : p + 1, :], (NT, 128))
            val = jnp.where((t < mute) | (t > NT - mute), adj[:, j * 128 : (j + 1) * 128], 0.0)
            rows = pl.ds(p, NT, stride=4)
            out_ref[rows, :] = direct_ref[rows, :] - val


def receiver_traces(pos, tables, mute, direct, x):
    return pl.pallas_call(
        receiver_kernel,
        in_specs=[SMEM] + [VMEM] * 5,
        out_specs=VMEM,
        out_shape=jax.ShapeDtypeStruct((NT * 4, 128), F32),
        compiler_params=params(8),
        name="receiver_traces",
    )(pos, *tables, mute, direct, x)


AROUND = ("xh", "xl", "y")
SWAP = [(0, 1), (1, 0)]


def exchange_xy(x):
    return lax.all_to_all(x, AROUND, split_axis=0, concat_axis=0, tiled=True)


def exchange_z(pieces):
    moved = [lax.ppermute(pieces[d], "z", [(i, (i + d) % 4) for i in range(4)]) for d in range(1, 4)]
    return [pieces[0]] + moved


def body(reflection, focusing, direct_wave, mute_source, mute_receiver):
    core, z, y = lax.axis_index("c"), lax.axis_index("z"), lax.axis_index("y")
    pos = jnp.stack([z, y, core, (z % 2) * 2 + lax.axis_index("xh")])
    table = dft_table()
    th, tl = split_const(table)

    focusing = pltpu.with_memory_space_constraint(focusing, pltpu.HBM)
    reflection = pltpu.with_memory_space_constraint(reflection, pltpu.HBM)
    own0, own1, oth0, oth1 = forward_panel(core.reshape(1), focusing, reflection)
    chains = []
    for own, oth in ((own0, oth0), (own1, oth1)):
        panel = own + lax.ppermute(oth, "c", SWAP)
        chains.append(exchange_z(sum_parts(pos, exchange_xy(panel))))
    time, b_own, b_oth = None, [], []
    for j in range(2):
        time, *back = source_traces(j, pos, (th, tl, th.T, tl.T), mute_source, chains[j], time)
        b_own.append(exchange_xy(spread(pos, exchange_z(back))))
        b_oth.append(lax.ppermute(b_own[j], "c", SWAP))
    adjoint = adjoint_panel(b_own, b_oth, reflection)
    received = lax.all_to_all(adjoint, ("z", "xh"), split_axis=0, concat_axis=0, tiled=True)
    plus = receiver_traces(pos, (th, tl), mute_receiver, direct_wave.reshape(NT * 4, 128), received)
    return time.reshape(NT, 2, 128), plus.reshape(NT, 4, 128)


def solution(mesh):
    fine = Mesh(mesh.devices.reshape(4, 2, 2, 4, 2), ("z", "xh", "xl", "y", "c"))
    freq, rcv = ("z", "xh"), ("xl", "y", "c")
    return jax.shard_map(
        body,
        mesh=fine,
        in_specs=(
            P(freq, None, None, rcv),
            P(freq, None, None, rcv),
            P(None, freq, rcv),
            P(rcv, freq),
            P(freq, rcv),
        ),
        out_specs=(P(None, rcv, freq), P(None, freq, rcv)),
        check_vma=False,
    )
```

```python
import math

import numpy as np
import jax
import jax.numpy as jnp
from jax import lax
from jax.experimental import pallas as pl
from jax.experimental.pallas import tpu as pltpu
from jax.sharding import Mesh, PartitionSpec as P

F32, BF16 = jnp.float32, jnp.bfloat16
NT = 256
KB, KK = 8, 16
VMEM = pl.BlockSpec(memory_space=pltpu.VMEM)
SMEM = pl.BlockSpec(memory_space=pltpu.SMEM)
HBM = pl.BlockSpec(memory_space=pltpu.HBM)


def dft_table():
    k = np.arange(1, KB * KK + 1)[None, :]
    t = np.arange(NT)[:, None]
    phase = 2.0 * math.pi * ((k * t) % NT) / NT
    c = 1.0 / math.sqrt(KB * KK)
    return np.stack([c * np.cos(phase), -c * np.sin(phase)], axis=2).reshape(NT, NT)


def split_const(table):
    high = table.astype(np.float32).astype(jnp.bfloat16)
    low = (table - high.astype(np.float64)).astype(np.float32).astype(jnp.bfloat16)
    return np.asarray(high), np.asarray(low)


def split(x):
    high = x.astype(BF16)
    return high, (x - high.astype(F32)).astype(BF16)


def mm(a, b, contract=(1, 0)):
    return lax.dot_general(a, b, (((contract[0],), (contract[1],)), ((), ())), preferred_element_type=F32)


def mm3(a, b):
    return mm(a[0], b[0]) + (mm(a[0], b[1]) + mm(a[1], b[0]))


def params(mib):
    return pltpu.CompilerParams(vmem_limit_bytes=mib * 2**20)


def trade(v, pair, shift):
    t = v[(0 - shift) % 4]
    for m in range(1, 4):
        t = jnp.where(pair == m, v[(m - shift) % 4], t)
    return t


def unturn(x, y, sign):
    out = x
    for s in range(1, 4):
        out = jnp.where(y == s, pltpu.roll(x, (sign * 2 * s) % 8, 1), out)
    return out


def forward_kernel(pos_ref, f_hbm, r_hbm, own, oth, rh_ref, rl_ref, f_ref, r_ref, fsem, sem):
    def fetch_f(g):
        cut = pl.ds(g * 4, 4)
        return pltpu.make_async_copy(f_hbm.at[cut], f_ref.at[cut], fsem.at[g])

    def fetch(g, z):
        cut = (pl.ds(g * 4, 4), slice(None), pl.ds(z * 256, 256))
        return pltpu.make_async_copy(r_hbm.at[cut], r_ref.at[cut], sem.at[g * 4 + z])

    fetch_f(0).start()
    for z in range(4):
        fetch(0, z).start()
    core = pos_ref[0]
    row = lax.broadcasted_iota(jnp.int32, (64, 64), 0)
    col = lax.broadcasted_iota(jnp.int32, (64, 64), 1)
    perms = []
    for q in range(4):
        c = (row // 32 + core) % 2
        y = ((row // 2) % 4 + 4 - q) % 4
        src = (row % 2) * 32 + ((row // 8) % 2) * 16 + y * 4 + c * 2 + (row // 16) % 2
        perms.append(jnp.where(col == src, 1.0, 0.0).astype(BF16))
    pair = lax.broadcasted_iota(jnp.int32, (8, 128), 0) // 2

    @pl.loop(0, 4)
    def _(g):
        fetch_f(g).wait()
        lhs = []
        for q in range(4):
            fr, fi = f_ref[g * 4 + q, 0], f_ref[g * 4 + q, 1]
            x = jnp.concatenate(
                [jnp.concatenate([fr, -fi], axis=1), jnp.concatenate([fi, fr], axis=1)], axis=0
            )
            xh, xl = split(x)
            ph, plo = mm(perms[q], xh).astype(BF16), mm(perms[q], xl).astype(BF16)
            lhs.append((ph, jnp.concatenate([ph, plo], axis=0)))
        g8 = pl.ds(pl.multiple_of(g * 8, 8), 8)

        @pl.when(g < 3)
        def _():
            fetch_f(g + 1).start()

        for z in range(4):
            fetch(g, z).wait()

            @pl.when(g < 3)
            def _():
                fetch(g + 1, z).start()

        for z in range(4):
            rows = slice(z * 256, (z + 1) * 256)
            res = []
            for q in range(4):
                k = g * 4 + q
                wh, wl = split(jnp.concatenate([r_ref[k, 0, rows, :], r_ref[k, 1, rows, :]], axis=1))
                rh_ref[k, rows, :] = wh
                rl_ref[k, rows, :] = wl
                acc = mm(lhs[q][1], wh, (1, 1))
                res.append(acc[:64] + (acc[64:] + mm(lhs[q][0], wl, (1, 1))))
            for xh_ in range(2):
                for part in range(8):
                    v = [r[part * 8 : part * 8 + 8, xh_ * 128 : xh_ * 128 + 128] for r in res]
                    out = oth if part // 4 else own
                    for y in range(4):
                        out[z * 2 + xh_, (part % 2) * 4 + y, (part // 2) % 2, g8, :] = trade(v, pair, y)


def forward_panel(pos, focusing, reflection):
    panel = jax.ShapeDtypeStruct((KB, 8, 2, 32, 128), F32)
    half = jax.ShapeDtypeStruct((KK, 1024, 256), BF16)
    return pl.pallas_call(
        forward_kernel,
        in_specs=[SMEM, HBM, HBM],
        out_specs=[VMEM] * 4,
        out_shape=[panel] * 2 + [half] * 2,
        scratch_shapes=[
            pltpu.VMEM((KK, 2, 32, 128), F32),
            pltpu.VMEM((KK, 2, 1024, 128), F32),
            pltpu.SemaphoreType.DMA((4,)),
            pltpu.SemaphoreType.DMA((16,)),
        ],
        compiler_params=params(24),
        cost_estimate=pl.CostEstimate(flops=3 * 2**30, bytes_accessed=21 * 2**20, transcendentals=0),
        name="forward_panel",
    )(pos, focusing, reflection)


def source_kernel(pos_ref, th_ref, tl_ref, tth_ref, ttl_ref, mute_ref, x_ref, time_ref, out_ref):
    y = pos_ref[2]
    cols = []
    for j in range(2):
        groups = []
        for f in range(KB):
            t = [x_ref[f, i, j] for i in range(8)]
            groups.append(((t[0] + t[1]) + (t[2] + t[3])) + ((t[4] + t[5]) + (t[6] + t[7])))
        x = jnp.concatenate(groups, axis=0)
        cols.append(unturn(x.reshape(32, 8, 128), y, -1).reshape(256, 128))
    up = mm3((th_ref[...], tl_ref[...]), split(jnp.concatenate(cols, axis=1)))
    t = lax.broadcasted_iota(jnp.int32, (NT, 128), 0)
    kept = []
    for j in range(2):
        mute = jnp.broadcast_to(mute_ref[j : j + 1, :], (NT, 128))
        val = jnp.where((t < mute) | (t > NT - mute), up[:, j * 128 : (j + 1) * 128], 0.0)
        time_ref[pl.ds(j, NT, stride=2), :] = val
        kept.append(val)
    back = mm3((tth_ref[...], ttl_ref[...]), split(jnp.concatenate(kept, axis=1)))
    for j in range(2):
        b = unturn(back[:, j * 128 : (j + 1) * 128].reshape(32, 8, 128), y, 1).reshape(KB, 32, 128)
        for f in range(KB):
            for i in range(8):
                out_ref[f, i, j] = b[f]


def source_traces(pos, tables, mute, parts):
    return pl.pallas_call(
        source_kernel,
        in_specs=[SMEM] + [VMEM] * 6,
        out_specs=[VMEM] * 2,
        out_shape=[
            jax.ShapeDtypeStruct((NT * 2, 128), F32),
            jax.ShapeDtypeStruct((KB, 8, 2, 32, 128), F32),
        ],
        compiler_params=params(8),
        name="source_traces",
    )(pos, *tables, mute, parts)


def adjoint_kernel(own, oth, rh_ref, rl_ref, out_ref):
    pair = lax.broadcasted_iota(jnp.int32, (8, 128), 0) // 2
    even = (lax.broadcasted_iota(jnp.int32, (64, 128), 0) % 2) == 0

    @pl.loop(0, 4)
    def _(g):
        g8 = pl.ds(pl.multiple_of(g * 8, 8), 8)
        acc = [None] * 4
        for z in range(4):
            lhs = [[None] * 2 for _ in range(4)]
            for xh_ in range(2):
                tiles = [[] for _ in range(4)]
                for part in range(8):
                    ref = oth if (part // 2) % 2 else own
                    v = [ref[z * 2 + xh_, (part % 2) * 4 + y, part // 4, g8, :] for y in range(4)]
                    for q in range(4):
                        tiles[q].append(trade(v, pair, q))
                for q in range(4):
                    lhs[q][xh_] = jnp.concatenate(tiles[q], axis=0)
            rows = slice(z * 256, (z + 1) * 256)
            for q in range(4):
                bh, bl = split(jnp.concatenate(lhs[q], axis=1))
                wh, wl = rh_ref[g * 4 + q, rows, :], rl_ref[g * 4 + q, rows, :]
                both = mm(jnp.concatenate([bh, bl], axis=0), wh)
                add = both[:64] + (both[64:] + mm(bh, wl))
                acc[q] = add if acc[q] is None else acc[q] + add
        res = []
        for q in range(4):
            a, b = acc[q][:, :128], acc[q][:, 128:]
            res.append(a + jnp.where(even, pltpu.roll(b, 63, 0), -pltpu.roll(b, 1, 0)))
        for part in range(8):
            v = [r[part * 8 : part * 8 + 8] for r in res]
            for y in range(4):
                out_ref[(part % 2) * 4 + y, part // 2, g8, :] = trade(v, pair, y)


def adjoint_panel(own, oth, rh, rl):
    return pl.pallas_call(
        adjoint_kernel,
        in_specs=[VMEM] * 4,
        out_specs=VMEM,
        out_shape=jax.ShapeDtypeStruct((8, 4, 32, 128), F32),
        compiler_params=params(8),
        cost_estimate=pl.CostEstimate(flops=3 * 2**30, bytes_accessed=2**20, transcendentals=0),
        name="adjoint_panel",
    )(own, oth, rh, rl)


def receiver_kernel(pos_ref, th_ref, tl_ref, mute_ref, direct_ref, x_ref, out_ref):
    even = pos_ref[0] == 0
    turn = pos_ref[1]
    t = lax.broadcasted_iota(jnp.int32, (NT, 128), 0)
    for c in range(2):
        cols = []
        for j in range(2):
            a = jnp.where(even, x_ref[:, j * 2 + c], x_ref[:, j * 2 + 1 - c])
            cols.append(unturn(a.reshape(32, 8, 128), turn, -1).reshape(256, 128))
        adj = mm3((th_ref[...], tl_ref[...]), split(jnp.concatenate(cols, axis=1)))
        for j in range(2):
            p = c * 2 + j
            mute = jnp.broadcast_to(mute_ref[p : p + 1, :], (NT, 128))
            val = jnp.where((t < mute) | (t > NT - mute), adj[:, j * 128 : (j + 1) * 128], 0.0)
            rows = pl.ds(p, NT, stride=4)
            out_ref[rows, :] = direct_ref[rows, :] - val


def receiver_traces(pos, tables, mute, direct, x):
    return pl.pallas_call(
        receiver_kernel,
        in_specs=[SMEM] + [VMEM] * 5,
        out_specs=VMEM,
        out_shape=jax.ShapeDtypeStruct((NT * 4, 128), F32),
        compiler_params=params(8),
        name="receiver_traces",
    )(pos, *tables, mute, direct, x)


CHIPS = ("z", "xh", "xl", "y")
SWAP = [(0, 1), (1, 0)]


def exchange(x, axes):
    whole = x.reshape((-1,) + x.shape[-3:]) if len(axes) == 4 else x
    return lax.all_to_all(whole, axes, split_axis=0, concat_axis=0, tiled=True).reshape(x.shape)


def body(reflection, focusing, direct_wave, mute_source, mute_receiver):
    core, z, y = lax.axis_index("c"), lax.axis_index("z"), lax.axis_index("y")
    pos = jnp.stack([core, (z & 1) * 2 + lax.axis_index("xh"), y])
    table = dft_table()
    th, tl = split_const(table)

    focusing = pltpu.with_memory_space_constraint(focusing, pltpu.HBM)
    reflection = pltpu.with_memory_space_constraint(reflection, pltpu.HBM)
    own, oth, rh, rl = forward_panel(pos, focusing, reflection)
    parts = exchange(own + lax.ppermute(oth, "c", SWAP), CHIPS)
    time, back = source_traces(pos, (th, tl, th.T, tl.T), mute_source, parts)
    b_own = exchange(back, CHIPS)
    b_oth = lax.ppermute(b_own, "c", SWAP)
    adjoint = adjoint_panel(b_own, b_oth, rh, rl)
    received = exchange(adjoint, ("z", "xh"))
    plus = receiver_traces(
        pos, (th, tl), mute_receiver, direct_wave.reshape(NT * 4, 128), received
    )
    return time.reshape(NT, 2, 128), plus.reshape(NT, 4, 128)


def solution(mesh):
    fine = Mesh(mesh.devices.reshape(4, 2, 2, 4, 2), ("z", "xh", "xl", "y", "c"))
    freq, rcv = ("z", "xh"), ("xl", "y", "c")
    return jax.shard_map(
        body,
        mesh=fine,
        in_specs=(
            P(freq, None, None, rcv),
            P(freq, None, None, rcv),
            P(None, freq, rcv),
            P(rcv, freq),
            P(freq, rcv),
        ),
        out_specs=(P(None, rcv, freq), P(None, freq, rcv)),
        check_vma=False,
    )
```

```python
import functools
import math

import numpy as np
import jax
import jax.numpy as jnp
from jax import lax
from jax.experimental import pallas as pl
from jax.experimental.pallas import tpu as pltpu
from jax.sharding import Mesh, PartitionSpec as P

F32, BF16 = jnp.float32, jnp.bfloat16
NT = 256
KB, KK = 8, 16
VMEM = pl.BlockSpec(memory_space=pltpu.VMEM)
SMEM = pl.BlockSpec(memory_space=pltpu.SMEM)
HBM = pl.BlockSpec(memory_space=pltpu.HBM)


def dft_table():
    k = np.arange(1, KB * KK + 1)[None, :]
    t = np.arange(NT)[:, None]
    phase = 2.0 * math.pi * ((k * t) % NT) / NT
    c = 1.0 / math.sqrt(KB * KK)
    return np.stack([c * np.cos(phase), -c * np.sin(phase)], axis=2).reshape(NT, NT)


def split_const(table):
    high = table.astype(np.float32).astype(jnp.bfloat16)
    low = (table - high.astype(np.float64)).astype(np.float32).astype(jnp.bfloat16)
    return np.asarray(high), np.asarray(low)


def split(x):
    high = x.astype(BF16)
    return high, (x - high.astype(F32)).astype(BF16)


def mm(a, b, contract=(1, 0)):
    return lax.dot_general(a, b, (((contract[0],), (contract[1],)), ((), ())), preferred_element_type=F32)


def mm3(a, b):
    return mm(a[0], b[0]) + (mm(a[0], b[1]) + mm(a[1], b[0]))


def params(mib):
    return pltpu.CompilerParams(vmem_limit_bytes=mib * 2**20)


def trade(v, pair, shift):
    t = v[(0 - shift) % 4]
    for m in range(1, 4):
        t = jnp.where(pair == m, v[(m - shift) % 4], t)
    return t


def unturn(x, y, sign):
    out = x
    for s in range(1, 4):
        out = jnp.where(y == s, pltpu.roll(x, (sign * 2 * s) % 8, 1), out)
    return out


def selections(core):
    row = lax.broadcasted_iota(jnp.int32, (64, 64), 0)
    col = lax.broadcasted_iota(jnp.int32, (64, 64), 1)
    out = []
    for q in range(4):
        c = (row // 32 + core) % 2
        y = ((row // 2) % 4 + 4 - q) % 4
        src = (row % 2) * 32 + ((row // 8) % 2) * 16 + y * 4 + c * 2 + (row // 16) % 2
        out.append(jnp.where(col == src, 1.0, 0.0).astype(BF16))
    return out


def group_operand(perms, f_ref, base):
    lhs = []
    for q in range(4):
        fr, fi = f_ref[base + q, 0], f_ref[base + q, 1]
        x = jnp.concatenate(
            [jnp.concatenate([fr, -fi], axis=1), jnp.concatenate([fi, fr], axis=1)], axis=0
        )
        xh, xl = split(x)
        ph, plo = mm(perms[q], xh).astype(BF16), mm(perms[q], xl).astype(BF16)
        lhs.append((ph, jnp.concatenate([ph, plo], axis=0)))
    return lhs


def group_block(g, z, lhs, r_ref, r_base, own, oth, rh_ref, rl_ref):
    pair = lax.broadcasted_iota(jnp.int32, (8, 128), 0) // 2
    rows = slice(z * 256, (z + 1) * 256)
    res = []
    for q in range(4):
        k = r_base + q
        wh, wl = split(jnp.concatenate([r_ref[k, 0, rows, :], r_ref[k, 1, rows, :]], axis=1))
        rh_ref[g * 4 + q, rows, :] = wh
        rl_ref[g * 4 + q, rows, :] = wl
        acc = mm(lhs[q][1], wh, (1, 1))
        res.append(acc[:64] + (acc[64:] + mm(lhs[q][0], wl, (1, 1))))
    for xh_ in range(2):
        for part in range(8):
            v = [r[part * 8 : part * 8 + 8, xh_ * 128 : xh_ * 128 + 128] for r in res]
            out = oth if part // 4 else own
            for y in range(4):
                out[z * 2 + xh_, (part % 2) * 4 + y, (part // 2) % 2, g * 8 : g * 8 + 8, :] = trade(
                    v, pair, y
                )


def forward_first_kernel(pos_ref, f_hbm, r_hbm, own, oth, rh, rl, ahead, f_ref, r_ref, fsem, sem, asem):
    def fetch_f(g):
        cut = pl.ds(g * 4, 4)
        return pltpu.make_async_copy(f_hbm.at[cut], f_ref.at[cut], fsem.at[g])

    def fetch(g, z):
        cut = (pl.ds(g * 4, 4), slice(None), pl.ds(z * 256, 256))
        return pltpu.make_async_copy(r_hbm.at[cut], r_ref.at[cut], sem.at[g * 4 + z])

    def fetch_ahead(k):
        return pltpu.make_async_copy(r_hbm.at[8 + k], ahead.at[k], asem.at[k])

    fetch_f(0).start()
    for z in range(4):
        fetch(0, z).start()
    fetch_f(1).start()
    perms = selections(pos_ref[0])
    fetch_f(0).wait()
    lhs = group_operand(perms, f_ref, 0)
    for z in range(4):
        fetch(0, z).wait()
        fetch(1, z).start()
        group_block(0, z, lhs, r_ref, 0, own, oth, rh, rl)
    fetch_f(1).wait()
    lhs = group_operand(perms, f_ref, 4)
    for z in range(4):
        fetch(1, z).wait()
        fetch_ahead(z).start()
    for z in range(4):
        group_block(1, z, lhs, r_ref, 4, own, oth, rh, rl)
    for k in range(4):
        fetch_ahead(k).wait()


def forward_second_kernel(pos_ref, f_hbm, r_hbm, ahead, own, oth, rh, rl, f_ref, r_ref, fsem, sem):
    def fetch(k):
        return pltpu.make_async_copy(r_hbm.at[12 + k], r_ref.at[k], sem.at[k])

    fcopy = pltpu.make_async_copy(f_hbm.at[pl.ds(8, 8)], f_ref, fsem)
    fcopy.start()
    for k in range(4):
        fetch(k).start()
    perms = selections(pos_ref[0])
    fcopy.wait()
    lhs = group_operand(perms, f_ref, 0)
    for z in range(4):
        group_block(0, z, lhs, ahead, 0, own, oth, rh, rl)
    lhs = group_operand(perms, f_ref, 4)
    for k in range(4):
        fetch(k).wait()
    for z in range(4):
        group_block(1, z, lhs, r_ref, 0, own, oth, rh, rl)


PANEL_HALF = jax.ShapeDtypeStruct((KB, 8, 2, 16, 128), F32)
R_HALF = jax.ShapeDtypeStruct((8, 1024, 256), BF16)
R_GROUP = (4, 2, 1024, 128)


def forward_first(pos, focusing, reflection):
    return pl.pallas_call(
        forward_first_kernel,
        in_specs=[SMEM, HBM, HBM],
        out_specs=[VMEM] * 5,
        out_shape=[PANEL_HALF] * 2 + [R_HALF] * 2 + [jax.ShapeDtypeStruct(R_GROUP, F32)],
        scratch_shapes=[
            pltpu.VMEM((8, 2, 32, 128), F32),
            pltpu.VMEM((8, 2, 1024, 128), F32),
            pltpu.SemaphoreType.DMA((2,)),
            pltpu.SemaphoreType.DMA((8,)),
            pltpu.SemaphoreType.DMA((4,)),
        ],
        compiler_params=params(16),
        cost_estimate=pl.CostEstimate(flops=3 * 2**29, bytes_accessed=14 * 2**20, transcendentals=0),
        name="forward_first",
    )(pos, focusing, reflection)


def forward_second(pos, focusing, reflection, ahead):
    return pl.pallas_call(
        forward_second_kernel,
        in_specs=[SMEM, HBM, HBM, VMEM],
        out_specs=[VMEM] * 4,
        out_shape=[PANEL_HALF] * 2 + [R_HALF] * 2,
        scratch_shapes=[
            pltpu.VMEM((8, 2, 32, 128), F32),
            pltpu.VMEM(R_GROUP, F32),
            pltpu.SemaphoreType.DMA,
            pltpu.SemaphoreType.DMA((4,)),
        ],
        compiler_params=params(12),
        cost_estimate=pl.CostEstimate(flops=3 * 2**29, bytes_accessed=10 * 2**20, transcendentals=0),
        name="forward_second",
    )(pos, focusing, reflection, ahead)


def combine_kernel(own0, oth0, own1, oth1, out_ref):
    out_ref[:, :, 0] = own0[...] + oth0[...]
    out_ref[:, :, 1] = own1[...] + oth1[...]


def combine(own0, oth0, own1, oth1):
    return pl.pallas_call(
        combine_kernel,
        in_specs=[VMEM] * 4,
        out_specs=VMEM,
        out_shape=jax.ShapeDtypeStruct((KB, 8, 2, 2, 16, 128), F32),
        compiler_params=params(4),
        name="combine",
    )(own0, oth0, own1, oth1)


def source_kernel(pos_ref, th_ref, tl_ref, tth_ref, ttl_ref, mute_ref, x_ref, time_ref, out_ref):
    y = pos_ref[2]
    cols = []
    for j in range(2):
        groups = []
        for f in range(KB):
            for h in range(2):
                t = [x_ref[f, i, h, j] for i in range(8)]
                groups.append(((t[0] + t[1]) + (t[2] + t[3])) + ((t[4] + t[5]) + (t[6] + t[7])))
        x = jnp.concatenate(groups, axis=0)
        cols.append(unturn(x.reshape(32, 8, 128), y, -1).reshape(256, 128))
    up = mm3((th_ref[...], tl_ref[...]), split(jnp.concatenate(cols, axis=1)))
    t = lax.broadcasted_iota(jnp.int32, (NT, 128), 0)
    kept = []
    for j in range(2):
        mute = jnp.broadcast_to(mute_ref[j : j + 1, :], (NT, 128))
        val = jnp.where((t < mute) | (t > NT - mute), up[:, j * 128 : (j + 1) * 128], 0.0)
        time_ref[pl.ds(j, NT, stride=2), :] = val
        kept.append(val)
    back = mm3((tth_ref[...], ttl_ref[...]), split(jnp.concatenate(kept, axis=1)))
    for j in range(2):
        b = unturn(back[:, j * 128 : (j + 1) * 128].reshape(32, 8, 128), y, 1)
        b = b.reshape(KB, 2, 16, 128)
        for f in range(KB):
            for h in range(2):
                for i in range(8):
                    out_ref[f, i, h, j] = b[f, h]


def source_traces(pos, tables, mute, parts):
    return pl.pallas_call(
        source_kernel,
        in_specs=[SMEM] + [VMEM] * 6,
        out_specs=[VMEM] * 2,
        out_shape=[
            jax.ShapeDtypeStruct((NT * 2, 128), F32),
            jax.ShapeDtypeStruct((KB, 8, 2, 2, 16, 128), F32),
        ],
        compiler_params=params(8),
        name="source_traces",
    )(pos, *tables, mute, parts)


def adjoint_kernel(second, own, oth, rh0, rl0, rh1, rl1, *rest):
    out_ref = rest[-1]
    pair = lax.broadcasted_iota(jnp.int32, (8, 128), 0) // 2
    even = (lax.broadcasted_iota(jnp.int32, (64, 128), 0) % 2) == 0
    for half, (rh_ref, rl_ref) in enumerate(((rh0, rl0), (rh1, rl1))):
        for g in range(2):
            acc = [None] * 4
            for zz in range(2):
                lhs = [[None] * 2 for _ in range(4)]
                for xh_ in range(2):
                    tiles = [[] for _ in range(4)]
                    f = zz * 2 + xh_
                    for part in range(8):
                        j, xlo = part // 4, part % 2
                        g8 = slice(g * 8, g * 8 + 8)
                        if (part // 2) % 2:
                            v = [oth[f, xlo * 4 + y, half, j, g8, :] for y in range(4)]
                        else:
                            v = [own[second * 4 + f, xlo * 4 + y, half, j, g8, :] for y in range(4)]
                        for q in range(4):
                            tiles[q].append(trade(v, pair, q))
                    for q in range(4):
                        lhs[q][xh_] = jnp.concatenate(tiles[q], axis=0)
                z = second * 2 + zz
                rows = slice(z * 256, (z + 1) * 256)
                for q in range(4):
                    bh, bl = split(jnp.concatenate(lhs[q], axis=1))
                    wh, wl = rh_ref[g * 4 + q, rows, :], rl_ref[g * 4 + q, rows, :]
                    both = mm(jnp.concatenate([bh, bl], axis=0), wh)
                    add = both[:64] + (both[64:] + mm(bh, wl))
                    acc[q] = add if acc[q] is None else acc[q] + add
            res = []
            for q in range(4):
                a, b = acc[q][:, :128], acc[q][:, 128:]
                res.append(a + jnp.where(even, pltpu.roll(b, 63, 0), -pltpu.roll(b, 1, 0)))
            out8 = slice(half * 16 + g * 8, half * 16 + g * 8 + 8)
            for part in range(8):
                v = [r[part * 8 : part * 8 + 8] for r in res]
                for y in range(4):
                    at = ((part % 2) * 4 + y, part // 2, out8, slice(None))
                    t = trade(v, pair, y)
                    out_ref[at] = rest[0][at] + t if second else t


def adjoint_panel(second, own, oth, halves, *before):
    return pl.pallas_call(
        functools.partial(adjoint_kernel, second),
        in_specs=[VMEM] * (6 + len(before)),
        out_specs=VMEM,
        out_shape=jax.ShapeDtypeStruct((8, 4, 32, 128), F32),
        compiler_params=params(8),
        cost_estimate=pl.CostEstimate(flops=3 * 2**29, bytes_accessed=2**20, transcendentals=0),
        name=f"adjoint_panel{second}",
    )(own, oth, *halves, *before)


def receiver_kernel(pos_ref, th_ref, tl_ref, mute_ref, direct_ref, x_ref, out_ref):
    even = pos_ref[0] == 0
    turn = pos_ref[1]
    t = lax.broadcasted_iota(jnp.int32, (NT, 128), 0)
    for c in range(2):
        cols = []
        for j in range(2):
            a = jnp.where(even, x_ref[:, j * 2 + c], x_ref[:, j * 2 + 1 - c])
            cols.append(unturn(a.reshape(32, 8, 128), turn, -1).reshape(256, 128))
        adj = mm3((th_ref[...], tl_ref[...]), split(jnp.concatenate(cols, axis=1)))
        for j in range(2):
            p = c * 2 + j
            mute = jnp.broadcast_to(mute_ref[p : p + 1, :], (NT, 128))
            val = jnp.where((t < mute) | (t > NT - mute), adj[:, j * 128 : (j + 1) * 128], 0.0)
            rows = pl.ds(p, NT, stride=4)
            out_ref[rows, :] = direct_ref[rows, :] - val


def receiver_traces(pos, tables, mute, direct, x):
    return pl.pallas_call(
        receiver_kernel,
        in_specs=[SMEM] + [VMEM] * 5,
        out_specs=VMEM,
        out_shape=jax.ShapeDtypeStruct((NT * 4, 128), F32),
        compiler_params=params(8),
        name="receiver_traces",
    )(pos, *tables, mute, direct, x)


CHIPS = ("z", "xh", "xl", "y")
SWAP = [(0, 1), (1, 0)]


def exchange(x, axes):
    whole = x.reshape((64,) + x.shape[2:]) if len(axes) == 4 else x
    return lax.all_to_all(whole, axes, split_axis=0, concat_axis=0, tiled=True).reshape(x.shape)


def body(reflection, focusing, direct_wave, mute_source, mute_receiver):
    core, z, y = lax.axis_index("c"), lax.axis_index("z"), lax.axis_index("y")
    pos = jnp.stack([core, (z & 1) * 2 + lax.axis_index("xh"), y])
    table = dft_table()
    th, tl = split_const(table)

    focusing = pltpu.with_memory_space_constraint(focusing, pltpu.HBM)
    reflection = pltpu.with_memory_space_constraint(reflection, pltpu.HBM)
    own0, oth0, rh0, rl0, ahead = forward_first(pos, focusing, reflection)
    own1, oth1, rh1, rl1 = forward_second(pos, focusing, reflection, ahead)
    panel = combine(own0, lax.ppermute(oth0, "c", SWAP), own1, lax.ppermute(oth1, "c", SWAP))
    parts = exchange(panel, CHIPS)
    time, back = source_traces(pos, (th, tl, th.T, tl.T), mute_source, parts)
    b_own = exchange(back, CHIPS)
    halves = (rh0, rl0, rh1, rl1)
    b_oth = [lax.ppermute(b_own[i * 4 : i * 4 + 4], "c", SWAP) for i in range(2)]
    adjoint = adjoint_panel(0, b_own, b_oth[0], halves)
    adjoint = adjoint_panel(1, b_own, b_oth[1], halves, adjoint)
    received = exchange(adjoint, ("z", "xh"))
    plus = receiver_traces(
        pos, (th, tl), mute_receiver, direct_wave.reshape(NT * 4, 128), received
    )
    return time.reshape(NT, 2, 128), plus.reshape(NT, 4, 128)


def solution(mesh):
    fine = Mesh(mesh.devices.reshape(4, 2, 2, 4, 2), ("z", "xh", "xl", "y", "c"))
    freq, rcv = ("z", "xh"), ("xl", "y", "c")
    return jax.shard_map(
        body,
        mesh=fine,
        in_specs=(
            P(freq, None, None, rcv),
            P(freq, None, None, rcv),
            P(None, freq, rcv),
            P(rcv, freq),
            P(freq, rcv),
        ),
        out_specs=(P(None, rcv, freq), P(None, freq, rcv)),
        check_vma=False,
    )
```

```python
import functools
import math

import numpy as np
import jax
import jax.numpy as jnp
from jax import lax
from jax.experimental import pallas as pl
from jax.experimental.pallas import tpu as pltpu
from jax.sharding import Mesh, PartitionSpec as P

F32, BF16 = jnp.float32, jnp.bfloat16
NT = 256
KB, KK = 8, 16
VMEM = pl.BlockSpec(memory_space=pltpu.VMEM)
SMEM = pl.BlockSpec(memory_space=pltpu.SMEM)
HBM = pl.BlockSpec(memory_space=pltpu.HBM)


def dft_table():
    k = np.arange(1, KB * KK + 1)[None, :]
    t = np.arange(NT)[:, None]
    phase = 2.0 * math.pi * ((k * t) % NT) / NT
    c = 1.0 / math.sqrt(KB * KK)
    return np.stack([c * np.cos(phase), -c * np.sin(phase)], axis=2).reshape(NT, NT)


def split_const(table):
    high = table.astype(np.float32).astype(jnp.bfloat16)
    low = (table - high.astype(np.float64)).astype(np.float32).astype(jnp.bfloat16)
    return np.asarray(high), np.asarray(low)


def split(x):
    high = x.astype(BF16)
    return high, (x - high.astype(F32)).astype(BF16)


def mm(a, b, contract=(1, 0)):
    return lax.dot_general(a, b, (((contract[0],), (contract[1],)), ((), ())), preferred_element_type=F32)


def mm3(a, b):
    return mm(a[0], b[0]) + (mm(a[0], b[1]) + mm(a[1], b[0]))


def params(mib):
    return pltpu.CompilerParams(vmem_limit_bytes=mib * 2**20)


def trade(v, pair, shift):
    t = v[(0 - shift) % 4]
    for m in range(1, 4):
        t = jnp.where(pair == m, v[(m - shift) % 4], t)
    return t


def unturn(x, y, sign):
    out = x
    for s in range(1, 4):
        out = jnp.where(y == s, pltpu.roll(x, (sign * 2 * s) % 8, 1), out)
    return out


def place(z, xh, xl, y):
    return z * 16 + ((xh * 2 + xl - y) % 4) * 4 + y


def place_groups():
    order = [None] * 64
    for z in range(4):
        for xh in range(2):
            for xl in range(2):
                for y in range(4):
                    order[place(z, xh, xl, y)] = ((z * 2 + xh) * 2 + xl) * 4 + y
    return [[chip * 2 + core for chip in order] for core in range(2)]


AHEAD = 6


def forward_kernel(pos_ref, f_hbm, r_hbm, own, oth, rh_ref, rl_ref, f_ref, r_ref, fsem, zsem, sem):
    def fetch_f(g):
        cut = pl.ds(g * 4, 4)
        return pltpu.make_async_copy(f_hbm.at[cut], f_ref.at[cut], fsem.at[g])

    def fetch_first(z):
        cut = (pl.ds(0, 4), slice(None), pl.ds(z * 256, 256))
        return pltpu.make_async_copy(r_hbm.at[cut], r_ref.at[cut], zsem.at[z])

    def fetch(k):
        return pltpu.make_async_copy(r_hbm.at[k], r_ref.at[k], sem.at[k - 4])

    fetch_f(0).start()
    for z in range(4):
        fetch_first(z).start()
    for k in range(4, AHEAD):
        fetch(k).start()
    for g in range(1, 4):
        fetch_f(g).start()
    core = pos_ref[0]
    row = lax.broadcasted_iota(jnp.int32, (64, 64), 0)
    col = lax.broadcasted_iota(jnp.int32, (64, 64), 1)
    perms = []
    for q in range(4):
        c = (row // 32 + core) % 2
        y = ((row // 2) % 4 + 4 - q) % 4
        src = (row % 2) * 32 + ((row // 8) % 2) * 16 + y * 4 + c * 2 + (row // 16) % 2
        perms.append(jnp.where(col == src, 1.0, 0.0).astype(BF16))
    pair = lax.broadcasted_iota(jnp.int32, (8, 128), 0) // 2

    def operands(g):
        lhs = []
        for q in range(4):
            fr, fi = f_ref[g * 4 + q, 0], f_ref[g * 4 + q, 1]
            x = jnp.concatenate(
                [jnp.concatenate([fr, -fi], axis=1), jnp.concatenate([fi, fr], axis=1)], axis=0
            )
            xh, xl = split(x)
            ph, plo = mm(perms[q], xh).astype(BF16), mm(perms[q], xl).astype(BF16)
            lhs.append((ph, jnp.concatenate([ph, plo], axis=0)))
        return lhs

    def block(g, g8, z, lhs):
        rows = slice(z * 256, (z + 1) * 256)
        res = []
        for q in range(4):
            k = g * 4 + q
            wh, wl = split(jnp.concatenate([r_ref[k, 0, rows, :], r_ref[k, 1, rows, :]], axis=1))
            rh_ref[k, rows, :] = wh
            rl_ref[k, rows, :] = wl
            acc = mm(lhs[q][1], wh, (1, 1))
            res.append(acc[:64] + (acc[64:] + mm(lhs[q][0], wl, (1, 1))))
        for xh_ in range(2):
            for part in range(8):
                v = [r[part * 8 : part * 8 + 8, xh_ * 128 : xh_ * 128 + 128] for r in res]
                out = oth if part // 4 else own
                for y in range(4):
                    out[place(z, xh_, part % 2, y), (part // 2) % 2, g8, :] = trade(v, pair, y)

    fetch_f(0).wait()
    lhs0 = operands(0)
    for z in range(4):
        fetch_first(z).wait()
        fetch(AHEAD + z).start()
        block(0, slice(0, 8), z, lhs0)

    @pl.loop(1, 4)
    def _(g):
        fetch_f(g).wait()
        lhs = operands(g)
        for q in range(4):
            k = g * 4 + q
            fetch(k).wait()

            @pl.when(k + AHEAD < KK)
            def _():
                fetch(k + AHEAD).start()

        for z in range(4):
            block(g, pl.ds(pl.multiple_of(g * 8, 8), 8), z, lhs)


def forward_panel(pos, focusing, reflection):
    panel = jax.ShapeDtypeStruct((64, 2, 32, 128), F32)
    half = jax.ShapeDtypeStruct((KK, 1024, 256), BF16)
    return pl.pallas_call(
        forward_kernel,
        in_specs=[SMEM, HBM, HBM],
        out_specs=[VMEM] * 4,
        out_shape=[panel] * 2 + [half] * 2,
        scratch_shapes=[
            pltpu.VMEM((KK, 2, 32, 128), F32),
            pltpu.VMEM((KK, 2, 1024, 128), F32),
            pltpu.SemaphoreType.DMA((4,)),
            pltpu.SemaphoreType.DMA((4,)),
            pltpu.SemaphoreType.DMA((12,)),
        ],
        compiler_params=params(24),
        cost_estimate=pl.CostEstimate(flops=3 * 2**30, bytes_accessed=21 * 2**20, transcendentals=0),
        name="forward_panel",
    )(pos, focusing, reflection)


def source_kernel(pos_ref, th_ref, tl_ref, tth_ref, ttl_ref, mute_ref, x_ref, time_ref, out_ref):
    turn = pos_ref[2]
    cols = []
    for j in range(2):
        groups = []
        for f in range(KB):
            t = [x_ref[place(f // 2, f % 2, i // 4, i % 4), j] for i in range(8)]
            groups.append(((t[0] + t[1]) + (t[2] + t[3])) + ((t[4] + t[5]) + (t[6] + t[7])))
        x = jnp.concatenate(groups, axis=0)
        cols.append(unturn(x.reshape(32, 8, 128), turn, -1).reshape(256, 128))
    up = mm3((th_ref[...], tl_ref[...]), split(jnp.concatenate(cols, axis=1)))
    t = lax.broadcasted_iota(jnp.int32, (NT, 128), 0)
    kept = []
    for j in range(2):
        mute = jnp.broadcast_to(mute_ref[j : j + 1, :], (NT, 128))
        val = jnp.where((t < mute) | (t > NT - mute), up[:, j * 128 : (j + 1) * 128], 0.0)
        time_ref[pl.ds(j, NT, stride=2), :] = val
        kept.append(val)
    back = mm3((tth_ref[...], ttl_ref[...]), split(jnp.concatenate(kept, axis=1)))
    for j in range(2):
        b = unturn(back[:, j * 128 : (j + 1) * 128].reshape(32, 8, 128), turn, 1)
        b = b.reshape(KB, 32, 128)
        for f in range(KB):
            for i in range(8):
                out_ref[place(f // 2, f % 2, i // 4, i % 4), j] = b[f]


def source_traces(pos, tables, mute, parts):
    return pl.pallas_call(
        source_kernel,
        in_specs=[SMEM] + [VMEM] * 6,
        out_specs=[VMEM] * 2,
        out_shape=[
            jax.ShapeDtypeStruct((NT * 2, 128), F32),
            jax.ShapeDtypeStruct((64, 2, 32, 128), F32),
        ],
        compiler_params=params(8),
        name="source_traces",
    )(pos, *tables, mute, parts)


def adjoint_kernel(second, own, oth, rh_ref, rl_ref, *rest):
    out_ref = rest[-1]
    pair = lax.broadcasted_iota(jnp.int32, (8, 128), 0) // 2
    even = (lax.broadcasted_iota(jnp.int32, (64, 128), 0) % 2) == 0

    @pl.loop(0, 4)
    def _(g):
        g8 = pl.ds(pl.multiple_of(g * 8, 8), 8)
        acc = [None] * 4
        for zz in range(2):
            z = second * 2 + zz
            lhs = [[None] * 2 for _ in range(4)]
            for xh_ in range(2):
                tiles = [[] for _ in range(4)]
                for part in range(8):
                    j, xlo = part // 4, part % 2
                    if (part // 2) % 2:
                        v = [oth[place(zz, xh_, xlo, y), j, g8, :] for y in range(4)]
                    else:
                        v = [own[place(z, xh_, xlo, y), j, g8, :] for y in range(4)]
                    for q in range(4):
                        tiles[q].append(trade(v, pair, q))
                for q in range(4):
                    lhs[q][xh_] = jnp.concatenate(tiles[q], axis=0)
            rows = slice(z * 256, (z + 1) * 256)
            for q in range(4):
                bh, bl = split(jnp.concatenate(lhs[q], axis=1))
                wh, wl = rh_ref[g * 4 + q, rows, :], rl_ref[g * 4 + q, rows, :]
                both = mm(jnp.concatenate([bh, bl], axis=0), wh)
                add = both[:64] + (both[64:] + mm(bh, wl))
                acc[q] = add if acc[q] is None else acc[q] + add
        res = []
        for q in range(4):
            a, b = acc[q][:, :128], acc[q][:, 128:]
            res.append(a + jnp.where(even, pltpu.roll(b, 63, 0), -pltpu.roll(b, 1, 0)))
        for part in range(8):
            v = [r[part * 8 : part * 8 + 8] for r in res]
            for y in range(4):
                at = ((part % 2) * 4 + y, part // 2, g8, slice(None))
                t = trade(v, pair, y)
                out_ref[at] = rest[0][at] + t if second else t


def adjoint_panel(second, own, oth, rh, rl, *before):
    return pl.pallas_call(
        functools.partial(adjoint_kernel, second),
        in_specs=[VMEM] * (4 + len(before)),
        out_specs=VMEM,
        out_shape=jax.ShapeDtypeStruct((8, 4, 32, 128), F32),
        compiler_params=params(8),
        cost_estimate=pl.CostEstimate(flops=3 * 2**29, bytes_accessed=2**20, transcendentals=0),
        name=f"adjoint_panel{second}",
    )(own, oth, rh, rl, *before)


def receiver_kernel(pos_ref, th_ref, tl_ref, mute_ref, direct_ref, x_ref, out_ref):
    even = pos_ref[0] == 0
    turn = pos_ref[1]
    t = lax.broadcasted_iota(jnp.int32, (NT, 128), 0)
    for c in range(2):
        cols = []
        for j in range(2):
            a = jnp.where(even, x_ref[:, j * 2 + c], x_ref[:, j * 2 + 1 - c])
            cols.append(unturn(a.reshape(32, 8, 128), turn, -1).reshape(256, 128))
        adj = mm3((th_ref[...], tl_ref[...]), split(jnp.concatenate(cols, axis=1)))
        for j in range(2):
            p = c * 2 + j
            mute = jnp.broadcast_to(mute_ref[p : p + 1, :], (NT, 128))
            val = jnp.where((t < mute) | (t > NT - mute), adj[:, j * 128 : (j + 1) * 128], 0.0)
            rows = pl.ds(p, NT, stride=4)
            out_ref[rows, :] = direct_ref[rows, :] - val


def receiver_traces(pos, tables, mute, direct, x):
    return pl.pallas_call(
        receiver_kernel,
        in_specs=[SMEM] + [VMEM] * 5,
        out_specs=VMEM,
        out_shape=jax.ShapeDtypeStruct((NT * 4, 128), F32),
        compiler_params=params(8),
        name="receiver_traces",
    )(pos, *tables, mute, direct, x)


SWAP = [(0, 1), (1, 0)]
EVERY = ("z", "xh", "xl", "y", "c")


def exchange(x):
    return lax.all_to_all(
        x, EVERY, split_axis=0, concat_axis=0, tiled=True, axis_index_groups=place_groups()
    )


def body(reflection, focusing, direct_wave, mute_source, mute_receiver):
    core, z, y = lax.axis_index("c"), lax.axis_index("z"), lax.axis_index("y")
    pos = jnp.stack([core, (z & 1) * 2 + lax.axis_index("xh"), y])
    table = dft_table()
    th, tl = split_const(table)

    focusing = pltpu.with_memory_space_constraint(focusing, pltpu.HBM)
    reflection = pltpu.with_memory_space_constraint(reflection, pltpu.HBM)
    own, oth, rh, rl = forward_panel(pos, focusing, reflection)
    parts = exchange(own + lax.ppermute(oth, "c", SWAP))
    time, back = source_traces(pos, (th, tl, th.T, tl.T), mute_source, parts)
    b_own = exchange(back)
    b_oth = [lax.ppermute(b_own[i * 32 : i * 32 + 32], "c", SWAP) for i in range(2)]
    adjoint = adjoint_panel(0, b_own, b_oth[0], rh, rl)
    adjoint = adjoint_panel(1, b_own, b_oth[1], rh, rl, adjoint)
    received = lax.all_to_all(adjoint, ("z", "xh"), split_axis=0, concat_axis=0, tiled=True)
    plus = receiver_traces(
        pos, (th, tl), mute_receiver, direct_wave.reshape(NT * 4, 128), received
    )
    return time.reshape(NT, 2, 128), plus.reshape(NT, 4, 128)


def solution(mesh):
    fine = Mesh(mesh.devices.reshape(4, 2, 2, 4, 2), ("z", "xh", "xl", "y", "c"))
    freq, rcv = ("z", "xh"), ("xl", "y", "c")
    return jax.shard_map(
        body,
        mesh=fine,
        in_specs=(
            P(freq, None, None, rcv),
            P(freq, None, None, rcv),
            P(None, freq, rcv),
            P(rcv, freq),
            P(freq, rcv),
        ),
        out_specs=(P(None, rcv, freq), P(None, freq, rcv)),
        check_vma=False,
    )
```

```python
import functools
import math

import numpy as np
import jax
import jax.numpy as jnp
from jax import lax
from jax.experimental import pallas as pl
from jax.experimental.pallas import tpu as pltpu
from jax.sharding import Mesh, PartitionSpec as P

F32, BF16 = jnp.float32, jnp.bfloat16
NT = 256
KB, KK = 8, 16
VMEM = pl.BlockSpec(memory_space=pltpu.VMEM)
SMEM = pl.BlockSpec(memory_space=pltpu.SMEM)
HBM = pl.BlockSpec(memory_space=pltpu.HBM)


def dft_table():
    k = np.arange(1, KB * KK + 1)[None, :]
    t = np.arange(NT)[:, None]
    phase = 2.0 * math.pi * ((k * t) % NT) / NT
    c = 1.0 / math.sqrt(KB * KK)
    return np.stack([c * np.cos(phase), -c * np.sin(phase)], axis=2).reshape(NT, NT)


def split_const(table):
    high = table.astype(np.float32).astype(jnp.bfloat16)
    low = (table - high.astype(np.float64)).astype(np.float32).astype(jnp.bfloat16)
    return np.asarray(high), np.asarray(low)


def split(x):
    high = x.astype(BF16)
    return high, (x - high.astype(F32)).astype(BF16)


def mm(a, b, contract=(1, 0)):
    return lax.dot_general(a, b, (((contract[0],), (contract[1],)), ((), ())), preferred_element_type=F32)


def mm3(a, b):
    return mm(a[0], b[0]) + (mm(a[0], b[1]) + mm(a[1], b[0]))


def params(mib):
    return pltpu.CompilerParams(vmem_limit_bytes=mib * 2**20)


def trade(v, pair, shift):
    t = v[(0 - shift) % 4]
    for m in range(1, 4):
        t = jnp.where(pair == m, v[(m - shift) % 4], t)
    return t


def unturn(x, y, sign):
    out = x
    for s in range(1, 4):
        out = jnp.where(y == s, pltpu.roll(x, (sign * 2 * s) % 8, 1), out)
    return out


def place(z, xh, xl, y):
    return z * 16 + ((xh * 2 + xl - y) % 4) * 4 + y


def place_groups():
    order = [None] * 64
    for z in range(4):
        for xh in range(2):
            for xl in range(2):
                for y in range(4):
                    order[place(z, xh, xl, y)] = ((z * 2 + xh) * 2 + xl) * 4 + y
    return [[chip * 2 + core for chip in order] for core in range(2)]


AHEAD = 6


def forward_kernel(pos_ref, f_hbm, r_hbm, own, oth, rh_ref, rl_ref, f_ref, r_ref, fsem, sem):
    def fetch_f(g):
        cut = pl.ds(g * 4, 4)
        return pltpu.make_async_copy(f_hbm.at[cut], f_ref.at[cut], fsem.at[g])

    def fetch(k):
        return pltpu.make_async_copy(r_hbm.at[k], r_ref.at[k], sem.at[k])

    fetch_f(0).start()
    for k in range(AHEAD):
        fetch(k).start()
    for g in range(1, 4):
        fetch_f(g).start()
    core = pos_ref[0]
    row = lax.broadcasted_iota(jnp.int32, (64, 64), 0)
    col = lax.broadcasted_iota(jnp.int32, (64, 64), 1)
    perms = []
    for q in range(4):
        c = (row // 32 + core) % 2
        y = ((row // 2) % 4 + 4 - q) % 4
        src = (row % 2) * 32 + ((row // 8) % 2) * 16 + y * 4 + c * 2 + (row // 16) % 2
        perms.append(jnp.where(col == src, 1.0, 0.0).astype(BF16))
    pair = lax.broadcasted_iota(jnp.int32, (8, 128), 0) // 2

    def operands(g):
        lhs = []
        for q in range(4):
            fr, fi = f_ref[g * 4 + q, 0], f_ref[g * 4 + q, 1]
            x = jnp.concatenate(
                [jnp.concatenate([fr, -fi], axis=1), jnp.concatenate([fi, fr], axis=1)], axis=0
            )
            xh, xl = split(x)
            ph, plo = mm(perms[q], xh).astype(BF16), mm(perms[q], xl).astype(BF16)
            lhs.append((ph, jnp.concatenate([ph, plo], axis=0)))
        return lhs

    def block(g, g8, z, lhs):
        rows = slice(z * 256, (z + 1) * 256)
        res = []
        for q in range(4):
            k = g * 4 + q
            wh, wl = split(jnp.concatenate([r_ref[k, 0, rows, :], r_ref[k, 1, rows, :]], axis=1))
            rh_ref[k, rows, :] = wh
            rl_ref[k, rows, :] = wl
            acc = mm(lhs[q][1], wh, (1, 1))
            res.append(acc[:64] + (acc[64:] + mm(lhs[q][0], wl, (1, 1))))
        for xh_ in range(2):
            for part in range(8):
                v = [r[part * 8 : part * 8 + 8, xh_ * 128 : xh_ * 128 + 128] for r in res]
                out = oth if part // 4 else own
                for y in range(4):
                    out[place(z, xh_, part % 2, y), (part // 2) % 2, g8, :] = trade(v, pair, y)

    @pl.loop(0, 4)
    def _(g):
        fetch_f(g).wait()
        lhs = operands(g)
        g8 = pl.ds(pl.multiple_of(g * 8, 8), 8)
        for q in range(4):
            k = g * 4 + q
            fetch(k).wait()

            @pl.when(k + AHEAD < KK)
            def _():
                fetch(k + AHEAD).start()

        for z in range(4):
            block(g, g8, z, lhs)


def forward_panel(pos, focusing, reflection):
    panel = jax.ShapeDtypeStruct((64, 2, 32, 128), F32)
    half = jax.ShapeDtypeStruct((KK, 1024, 256), BF16)
    return pl.pallas_call(
        forward_kernel,
        in_specs=[SMEM, HBM, HBM],
        out_specs=[VMEM] * 4,
        out_shape=[panel] * 2 + [half] * 2,
        scratch_shapes=[
            pltpu.VMEM((KK, 2, 32, 128), F32),
            pltpu.VMEM((KK, 2, 1024, 128), F32),
            pltpu.SemaphoreType.DMA((4,)),
            pltpu.SemaphoreType.DMA((16,)),
        ],
        compiler_params=params(24),
        cost_estimate=pl.CostEstimate(flops=3 * 2**30, bytes_accessed=21 * 2**20, transcendentals=0),
        name="forward_panel",
    )(pos, focusing, reflection)


def source_kernel(pos_ref, th_ref, tl_ref, tth_ref, ttl_ref, mute_ref, x_ref, time_ref, out_ref):
    turn = pos_ref[2]
    cols = []
    for j in range(2):
        groups = []
        for f in range(KB):
            t = [x_ref[place(f // 2, f % 2, i // 4, i % 4), j] for i in range(8)]
            groups.append(((t[0] + t[1]) + (t[2] + t[3])) + ((t[4] + t[5]) + (t[6] + t[7])))
        x = jnp.concatenate(groups, axis=0)
        cols.append(unturn(x.reshape(32, 8, 128), turn, -1).reshape(256, 128))
    up = mm3((th_ref[...], tl_ref[...]), split(jnp.concatenate(cols, axis=1)))
    t = lax.broadcasted_iota(jnp.int32, (NT, 128), 0)
    kept = []
    for j in range(2):
        mute = jnp.broadcast_to(mute_ref[j : j + 1, :], (NT, 128))
        val = jnp.where((t < mute) | (t > NT - mute), up[:, j * 128 : (j + 1) * 128], 0.0)
        time_ref[pl.ds(j, NT, stride=2), :] = val
        kept.append(val)
    back = mm3((tth_ref[...], ttl_ref[...]), split(jnp.concatenate(kept, axis=1)))
    for j in range(2):
        b = unturn(back[:, j * 128 : (j + 1) * 128].reshape(32, 8, 128), turn, 1)
        b = b.reshape(KB, 32, 128)
        for f in range(KB):
            for i in range(8):
                out_ref[place(f // 2, f % 2, i // 4, i % 4), j] = b[f]


def source_traces(pos, tables, mute, parts):
    return pl.pallas_call(
        source_kernel,
        in_specs=[SMEM] + [VMEM] * 6,
        out_specs=[VMEM] * 2,
        out_shape=[
            jax.ShapeDtypeStruct((NT * 2, 128), F32),
            jax.ShapeDtypeStruct((64, 2, 32, 128), F32),
        ],
        compiler_params=params(8),
        name="source_traces",
    )(pos, *tables, mute, parts)


def adjoint_kernel(second, own, oth, rh_ref, rl_ref, *rest):
    out_ref = rest[-1]
    pair = lax.broadcasted_iota(jnp.int32, (8, 128), 0) // 2
    even = (lax.broadcasted_iota(jnp.int32, (64, 128), 0) % 2) == 0

    for g in range(4):
        g8 = slice(g * 8, g * 8 + 8)
        acc = [None] * 4
        for zz in range(2):
            z = second * 2 + zz
            lhs = [[None] * 2 for _ in range(4)]
            for xh_ in range(2):
                tiles = [[] for _ in range(4)]
                for part in range(8):
                    j, xlo = part // 4, part % 2
                    if (part // 2) % 2:
                        v = [oth[place(zz, xh_, xlo, y), j, g8, :] for y in range(4)]
                    else:
                        v = [own[place(z, xh_, xlo, y), j, g8, :] for y in range(4)]
                    for q in range(4):
                        tiles[q].append(trade(v, pair, q))
                for q in range(4):
                    lhs[q][xh_] = jnp.concatenate(tiles[q], axis=0)
            rows = slice(z * 256, (z + 1) * 256)
            for q in range(4):
                bh, bl = split(jnp.concatenate(lhs[q], axis=1))
                wh, wl = rh_ref[g * 4 + q, rows, :], rl_ref[g * 4 + q, rows, :]
                both = mm(jnp.concatenate([bh, bl], axis=0), wh)
                add = both[:64] + (both[64:] + mm(bh, wl))
                acc[q] = add if acc[q] is None else acc[q] + add
        res = []
        for q in range(4):
            a, b = acc[q][:, :128], acc[q][:, 128:]
            res.append(a + jnp.where(even, pltpu.roll(b, 63, 0), -pltpu.roll(b, 1, 0)))
        for part in range(8):
            v = [r[part * 8 : part * 8 + 8] for r in res]
            for y in range(4):
                at = ((part % 2) * 4 + y, part // 2, g8, slice(None))
                t = trade(v, pair, y)
                out_ref[at] = rest[0][at] + t if second else t


def adjoint_panel(second, own, oth, rh, rl, *before):
    return pl.pallas_call(
        functools.partial(adjoint_kernel, second),
        in_specs=[VMEM] * (4 + len(before)),
        out_specs=VMEM,
        out_shape=jax.ShapeDtypeStruct((8, 4, 32, 128), F32),
        compiler_params=params(8),
        cost_estimate=pl.CostEstimate(flops=3 * 2**29, bytes_accessed=2**20, transcendentals=0),
        name=f"adjoint_panel{second}",
    )(own, oth, rh, rl, *before)


def receiver_kernel(pos_ref, th_ref, tl_ref, mute_ref, direct_ref, x_ref, out_ref, high, low):
    step = pl.program_id(0)
    t = lax.broadcasted_iota(jnp.int32, (NT // 2, 128), 0) + step * (NT // 2)

    @pl.when(step == 0)
    def _():
        even = pos_ref[0] == 0
        turn = pos_ref[1]
        for p in range(4):
            c, j = p // 2, p % 2
            a = jnp.where(even, x_ref[:, j * 2 + c], x_ref[:, j * 2 + 1 - c])
            a = unturn(a.reshape(32, 8, 128), turn, -1).reshape(256, 128)
            high[:, p * 128 : p * 128 + 128], low[:, p * 128 : p * 128 + 128] = split(a)

    adj = mm3((th_ref[...], tl_ref[...]), (high[...], low[...]))
    for p in range(4):
        mute = jnp.broadcast_to(mute_ref[p : p + 1, :], (NT // 2, 128))
        val = jnp.where((t < mute) | (t > NT - mute), adj[:, p * 128 : (p + 1) * 128], 0.0)
        rows = pl.ds(p, NT // 2, stride=4)
        out_ref[rows, :] = direct_ref[rows, :] - val


def receiver_traces(pos, tables, mute, direct, x):
    half = pl.BlockSpec((NT // 2, NT), lambda i: (i, 0))
    rows = pl.BlockSpec((NT * 2, 128), lambda i: (i, 0))
    return pl.pallas_call(
        receiver_kernel,
        grid=(2,),
        in_specs=[SMEM, half, half, VMEM, rows, VMEM],
        out_specs=rows,
        out_shape=jax.ShapeDtypeStruct((NT * 4, 128), F32),
        scratch_shapes=[pltpu.VMEM((NT, 512), BF16)] * 2,
        compiler_params=params(8),
        name="receiver_traces",
    )(pos, *tables, mute, direct, x)


SWAP = [(0, 1), (1, 0)]
EVERY = ("z", "xh", "xl", "y", "c")


def exchange(x):
    return lax.all_to_all(
        x, EVERY, split_axis=0, concat_axis=0, tiled=True, axis_index_groups=place_groups()
    )


def body(reflection, focusing, direct_wave, mute_source, mute_receiver):
    core, z, y = lax.axis_index("c"), lax.axis_index("z"), lax.axis_index("y")
    pos = jnp.stack([core, (z & 1) * 2 + lax.axis_index("xh"), y])
    table = dft_table()
    th, tl = split_const(table)

    focusing = pltpu.with_memory_space_constraint(focusing, pltpu.HBM)
    reflection = pltpu.with_memory_space_constraint(reflection, pltpu.HBM)
    own, oth, rh, rl = forward_panel(pos, focusing, reflection)
    parts = exchange(own + lax.ppermute(oth, "c", SWAP))
    time, back = source_traces(pos, (th, tl, th.T, tl.T), mute_source, parts)
    b_own = exchange(back)
    b_oth = [lax.ppermute(b_own[i * 32 : i * 32 + 32], "c", SWAP) for i in range(2)]
    adjoint = adjoint_panel(0, b_own, b_oth[0], rh, rl)
    adjoint = adjoint_panel(1, b_own, b_oth[1], rh, rl, adjoint)
    received = lax.all_to_all(adjoint, ("z", "xh"), split_axis=0, concat_axis=0, tiled=True)
    plus = receiver_traces(
        pos, (th, tl), mute_receiver, direct_wave.reshape(NT * 4, 128), received
    )
    return time.reshape(NT, 2, 128), plus.reshape(NT, 4, 128)


def solution(mesh):
    fine = Mesh(mesh.devices.reshape(4, 2, 2, 4, 2), ("z", "xh", "xl", "y", "c"))
    freq, rcv = ("z", "xh"), ("xl", "y", "c")
    return jax.shard_map(
        body,
        mesh=fine,
        in_specs=(
            P(freq, None, None, rcv),
            P(freq, None, None, rcv),
            P(None, freq, rcv),
            P(rcv, freq),
            P(freq, rcv),
        ),
        out_specs=(P(None, rcv, freq), P(None, freq, rcv)),
        check_vma=False,
    )
```

```python
import functools
import math

import numpy as np
import jax
import jax.numpy as jnp
from jax import lax
from jax.experimental import pallas as pl
from jax.experimental.pallas import tpu as pltpu
from jax.sharding import Mesh, PartitionSpec as P

F32, BF16 = jnp.float32, jnp.bfloat16
NT = 256
KB, KK = 8, 16
VMEM = pl.BlockSpec(memory_space=pltpu.VMEM)
SMEM = pl.BlockSpec(memory_space=pltpu.SMEM)
HBM = pl.BlockSpec(memory_space=pltpu.HBM)


def dft_table():
    k = np.arange(1, KB * KK + 1)[None, :]
    t = np.arange(NT)[:, None]
    phase = 2.0 * math.pi * ((k * t) % NT) / NT
    c = 1.0 / math.sqrt(KB * KK)
    return np.stack([c * np.cos(phase), -c * np.sin(phase)], axis=2).reshape(NT, NT)


def split_const(table):
    high = table.astype(np.float32).astype(jnp.bfloat16)
    low = (table - high.astype(np.float64)).astype(np.float32).astype(jnp.bfloat16)
    return np.asarray(high), np.asarray(low)


def split(x):
    high = x.astype(BF16)
    return high, (x - high.astype(F32)).astype(BF16)


def mm(a, b, contract=(1, 0)):
    return lax.dot_general(a, b, (((contract[0],), (contract[1],)), ((), ())), preferred_element_type=F32)


def mm3(a, b):
    return mm(a[0], b[0]) + (mm(a[0], b[1]) + mm(a[1], b[0]))


def params(mib):
    return pltpu.CompilerParams(vmem_limit_bytes=mib * 2**20)


def trade(v, pair, shift):
    t = v[(0 - shift) % 4]
    for m in range(1, 4):
        t = jnp.where(pair == m, v[(m - shift) % 4], t)
    return t


def unturn(x, y, sign):
    out = x
    for s in range(1, 4):
        out = jnp.where(y == s, pltpu.roll(x, (sign * 2 * s) % 8, 1), out)
    return out


def place(z, xh, xl, y):
    return z * 16 + ((xh * 2 + xl - y) % 4) * 4 + y


def place_groups():
    order = [None] * 64
    for z in range(4):
        for xh in range(2):
            for xl in range(2):
                for y in range(4):
                    order[place(z, xh, xl, y)] = ((z * 2 + xh) * 2 + xl) * 4 + y
    return [[chip * 2 + core for chip in order] for core in range(2)]


AHEAD = 7


def forward_kernel(pos_ref, f_hbm, r_hbm, own, oth, rh_ref, rl_ref, f_ref, r_ref, fsem, sem):
    def fetch_f(g):
        cut = pl.ds(g * 4, 4)
        return pltpu.make_async_copy(f_hbm.at[cut], f_ref.at[cut], fsem.at[g])

    def fetch(k):
        return pltpu.make_async_copy(r_hbm.at[k], r_ref.at[k], sem.at[k])

    fetch_f(0).start()
    for k in range(AHEAD):
        fetch(k).start()
    for g in range(1, 4):
        fetch_f(g).start()
    core = pos_ref[0]
    row = lax.broadcasted_iota(jnp.int32, (64, 64), 0)
    col = lax.broadcasted_iota(jnp.int32, (64, 64), 1)
    perms = []
    for q in range(4):
        c = (row // 32 + core) % 2
        y = ((row // 2) % 4 + 4 - q) % 4
        src = (row % 2) * 32 + ((row // 8) % 2) * 16 + y * 4 + c * 2 + (row // 16) % 2
        perms.append(jnp.where(col == src, 1.0, 0.0).astype(BF16))
    pair = lax.broadcasted_iota(jnp.int32, (8, 128), 0) // 2

    def operands(g):
        lhs = []
        for q in range(4):
            fr, fi = f_ref[g * 4 + q, 0], f_ref[g * 4 + q, 1]
            x = jnp.concatenate(
                [jnp.concatenate([fr, -fi], axis=1), jnp.concatenate([fi, fr], axis=1)], axis=0
            )
            xh, xl = split(x)
            ph, plo = mm(perms[q], xh).astype(BF16), mm(perms[q], xl).astype(BF16)
            lhs.append((ph, jnp.concatenate([ph, plo], axis=0)))
        return lhs

    def block(g, g8, z, lhs):
        rows = slice(z * 256, (z + 1) * 256)
        res = []
        for q in range(4):
            k = g * 4 + q
            wh, wl = split(jnp.concatenate([r_ref[k, 0, rows, :], r_ref[k, 1, rows, :]], axis=1))
            rh_ref[k, rows, :] = wh
            rl_ref[k, rows, :] = wl
            if q % 2:
                low = jnp.concatenate([lhs[q][0], jnp.zeros_like(lhs[q][0])], axis=0)
                acc = (mm(wh, lhs[q][1], (1, 1)) + mm(wl, low, (1, 1))).T
                res.append(acc[:64] + acc[64:])
            else:
                acc = mm(lhs[q][1], wh, (1, 1))
                res.append(acc[:64] + (acc[64:] + mm(lhs[q][0], wl, (1, 1))))
        for xh_ in range(2):
            for part in range(8):
                v = [r[part * 8 : part * 8 + 8, xh_ * 128 : xh_ * 128 + 128] for r in res]
                out = oth if part // 4 else own
                for y in range(4):
                    out[place(z, xh_, part % 2, y), (part // 2) % 2, g8, :] = trade(v, pair, y)

    @pl.loop(0, 4)
    def _(g):
        fetch_f(g).wait()
        lhs = operands(g)
        g8 = pl.ds(pl.multiple_of(g * 8, 8), 8)
        for q in range(4):
            k = g * 4 + q
            fetch(k).wait()

            @pl.when(k + AHEAD < KK)
            def _():
                fetch(k + AHEAD).start()

        for z in range(4):
            block(g, g8, z, lhs)


def forward_panel(pos, focusing, reflection):
    panel = jax.ShapeDtypeStruct((64, 2, 32, 128), F32)
    half = jax.ShapeDtypeStruct((KK, 1024, 256), BF16)
    return pl.pallas_call(
        forward_kernel,
        in_specs=[SMEM, HBM, HBM],
        out_specs=[VMEM] * 4,
        out_shape=[panel] * 2 + [half] * 2,
        scratch_shapes=[
            pltpu.VMEM((KK, 2, 32, 128), F32),
            pltpu.VMEM((KK, 2, 1024, 128), F32),
            pltpu.SemaphoreType.DMA((4,)),
            pltpu.SemaphoreType.DMA((16,)),
        ],
        compiler_params=params(24),
        cost_estimate=pl.CostEstimate(flops=3 * 2**30, bytes_accessed=21 * 2**20, transcendentals=0),
        name="forward_panel",
    )(pos, focusing, reflection)


def source_kernel(pos_ref, th_ref, tl_ref, tth_ref, ttl_ref, mute_ref, x_ref, time_hbm, out_ref, time_ref, sem):
    turn = pos_ref[2]
    cols = []
    for j in range(2):
        groups = []
        for f in range(KB):
            t = [x_ref[place(f // 2, f % 2, i // 4, i % 4), j] for i in range(8)]
            groups.append(((t[0] + t[1]) + (t[2] + t[3])) + ((t[4] + t[5]) + (t[6] + t[7])))
        x = jnp.concatenate(groups, axis=0)
        cols.append(unturn(x.reshape(32, 8, 128), turn, -1).reshape(256, 128))
    up = mm3((th_ref[...], tl_ref[...]), split(jnp.concatenate(cols, axis=1)))
    t = lax.broadcasted_iota(jnp.int32, (NT, 128), 0)
    kept = []
    for j in range(2):
        mute = jnp.broadcast_to(mute_ref[j : j + 1, :], (NT, 128))
        val = jnp.where((t < mute) | (t > NT - mute), up[:, j * 128 : (j + 1) * 128], 0.0)
        time_ref[pl.ds(j, NT, stride=2), :] = val
        kept.append(val)
    copy = pltpu.make_async_copy(time_ref, time_hbm, sem)
    copy.start()
    back = mm3((tth_ref[...], ttl_ref[...]), split(jnp.concatenate(kept, axis=1)))
    for j in range(2):
        b = unturn(back[:, j * 128 : (j + 1) * 128].reshape(32, 8, 128), turn, 1)
        b = b.reshape(KB, 32, 128)
        for f in range(KB):
            for i in range(8):
                out_ref[place(f // 2, f % 2, i // 4, i % 4), j] = b[f]
    copy.wait()


def source_traces(pos, tables, mute, parts):
    return pl.pallas_call(
        source_kernel,
        in_specs=[SMEM] + [VMEM] * 6,
        out_specs=[HBM, VMEM],
        out_shape=[
            jax.ShapeDtypeStruct((NT * 2, 128), F32),
            jax.ShapeDtypeStruct((64, 2, 32, 128), F32),
        ],
        scratch_shapes=[pltpu.VMEM((NT * 2, 128), F32), pltpu.SemaphoreType.DMA],
        compiler_params=params(8),
        name="source_traces",
    )(pos, *tables, mute, parts)


def adjoint_kernel(second, own, oth, rh_ref, rl_ref, *rest):
    out_ref = rest[-1]
    pair = lax.broadcasted_iota(jnp.int32, (8, 128), 0) // 2
    even = (lax.broadcasted_iota(jnp.int32, (64, 128), 0) % 2) == 0

    for g in range(4):
        g8 = slice(g * 8, g * 8 + 8)
        acc = [None] * 4
        for zz in range(2):
            z = second * 2 + zz
            lhs = [[None] * 2 for _ in range(4)]
            for xh_ in range(2):
                tiles = [[] for _ in range(4)]
                for part in range(8):
                    j, xlo = part // 4, part % 2
                    if (part // 2) % 2:
                        v = [oth[place(zz, xh_, xlo, y), j, g8, :] for y in range(4)]
                    else:
                        v = [own[place(z, xh_, xlo, y), j, g8, :] for y in range(4)]
                    for q in range(4):
                        tiles[q].append(trade(v, pair, q))
                for q in range(4):
                    lhs[q][xh_] = jnp.concatenate(tiles[q], axis=0)
            rows = slice(z * 256, (z + 1) * 256)
            for q in range(4):
                bh, bl = split(jnp.concatenate(lhs[q], axis=1))
                wh, wl = rh_ref[g * 4 + q, rows, :], rl_ref[g * 4 + q, rows, :]
                both = mm(jnp.concatenate([bh, bl], axis=0), wh)
                add = both[:64] + (both[64:] + mm(bh, wl))
                acc[q] = add if acc[q] is None else acc[q] + add
        res = []
        for q in range(4):
            a, b = acc[q][:, :128], acc[q][:, 128:]
            res.append(a + jnp.where(even, pltpu.roll(b, 63, 0), -pltpu.roll(b, 1, 0)))
        for part in range(8):
            v = [r[part * 8 : part * 8 + 8] for r in res]
            for y in range(4):
                at = ((part % 2) * 4 + y, part // 2, g8, slice(None))
                t = trade(v, pair, y)
                out_ref[at] = rest[0][at] + t if second else t


def adjoint_panel(second, own, oth, rh, rl, *before):
    return pl.pallas_call(
        functools.partial(adjoint_kernel, second),
        in_specs=[VMEM] * (4 + len(before)),
        out_specs=VMEM,
        out_shape=jax.ShapeDtypeStruct((8, 4, 32, 128), F32),
        compiler_params=params(8),
        cost_estimate=pl.CostEstimate(flops=3 * 2**29, bytes_accessed=2**20, transcendentals=0),
        name=f"adjoint_panel{second}",
    )(own, oth, rh, rl, *before)


def receiver_kernel(pos_ref, th_ref, tl_ref, mute_ref, direct_ref, x_ref, out_ref):
    even = pos_ref[0] == 0
    turn = pos_ref[1]
    t = lax.broadcasted_iota(jnp.int32, (NT, 128), 0)
    for c in range(2):
        cols = []
        for j in range(2):
            a = jnp.where(even, x_ref[:, j * 2 + c], x_ref[:, j * 2 + 1 - c])
            cols.append(unturn(a.reshape(32, 8, 128), turn, -1).reshape(256, 128))
        adj = mm3((th_ref[...], tl_ref[...]), split(jnp.concatenate(cols, axis=1)))
        for j in range(2):
            p = c * 2 + j
            mute = jnp.broadcast_to(mute_ref[p : p + 1, :], (NT, 128))
            val = jnp.where((t < mute) | (t > NT - mute), adj[:, j * 128 : (j + 1) * 128], 0.0)
            rows = pl.ds(p, NT, stride=4)
            out_ref[rows, :] = direct_ref[rows, :] - val


def receiver_traces(pos, tables, mute, direct, x):
    return pl.pallas_call(
        receiver_kernel,
        in_specs=[SMEM] + [VMEM] * 5,
        out_specs=VMEM,
        out_shape=jax.ShapeDtypeStruct((NT * 4, 128), F32),
        compiler_params=params(8),
        name="receiver_traces",
    )(pos, *tables, mute, direct, x)


SWAP = [(0, 1), (1, 0)]
EVERY = ("z", "xh", "xl", "y", "c")


def exchange(x):
    return lax.all_to_all(
        x, EVERY, split_axis=0, concat_axis=0, tiled=True, axis_index_groups=place_groups()
    )


def body(reflection, focusing, direct_wave, mute_source, mute_receiver):
    core, z, y = lax.axis_index("c"), lax.axis_index("z"), lax.axis_index("y")
    pos = jnp.stack([core, (z & 1) * 2 + lax.axis_index("xh"), y])
    table = dft_table()
    th, tl = split_const(table)

    focusing = pltpu.with_memory_space_constraint(focusing, pltpu.HBM)
    reflection = pltpu.with_memory_space_constraint(reflection, pltpu.HBM)
    own, oth, rh, rl = forward_panel(pos, focusing, reflection)
    parts = exchange(own + lax.ppermute(oth, "c", SWAP))
    time, back = source_traces(pos, (th, tl, th.T, tl.T), mute_source, parts)
    b_own = exchange(back)
    b_oth = [lax.ppermute(b_own[i * 32 : i * 32 + 32], "c", SWAP) for i in range(2)]
    adjoint = adjoint_panel(0, b_own, b_oth[0], rh, rl)
    adjoint = adjoint_panel(1, b_own, b_oth[1], rh, rl, adjoint)
    received = lax.all_to_all(adjoint, ("z", "xh"), split_axis=0, concat_axis=0, tiled=True)
    plus = receiver_traces(
        pos, (th, tl), mute_receiver, direct_wave.reshape(NT * 4, 128), received
    )
    return time.reshape(NT, 2, 128), plus.reshape(NT, 4, 128)


def solution(mesh):
    fine = Mesh(mesh.devices.reshape(4, 2, 2, 4, 2), ("z", "xh", "xl", "y", "c"))
    freq, rcv = ("z", "xh"), ("xl", "y", "c")
    return jax.shard_map(
        body,
        mesh=fine,
        in_specs=(
            P(freq, None, None, rcv),
            P(freq, None, None, rcv),
            P(None, freq, rcv),
            P(rcv, freq),
            P(freq, rcv),
        ),
        out_specs=(P(None, rcv, freq), P(None, freq, rcv)),
        check_vma=False,
    )
```

```python
import functools
import math

import numpy as np
import jax
import jax.numpy as jnp
from jax import lax
from jax.experimental import pallas as pl
from jax.experimental.pallas import tpu as pltpu
from jax.sharding import Mesh, PartitionSpec as P

F32, BF16 = jnp.float32, jnp.bfloat16
NT = 256
KB, KK = 8, 16
VMEM = pl.BlockSpec(memory_space=pltpu.VMEM)
SMEM = pl.BlockSpec(memory_space=pltpu.SMEM)
HBM = pl.BlockSpec(memory_space=pltpu.HBM)


def dft_table():
    k = np.arange(1, KB * KK + 1)[None, :]
    t = np.arange(NT)[:, None]
    phase = 2.0 * math.pi * ((k * t) % NT) / NT
    c = 1.0 / math.sqrt(KB * KK)
    return np.stack([c * np.cos(phase), -c * np.sin(phase)], axis=2).reshape(NT, NT)


def split_const(table):
    high = table.astype(np.float32).astype(jnp.bfloat16)
    low = (table - high.astype(np.float64)).astype(np.float32).astype(jnp.bfloat16)
    return np.asarray(high), np.asarray(low)


def split(x):
    high = x.astype(BF16)
    return high, (x - high.astype(F32)).astype(BF16)


def mm(a, b, contract=(1, 0)):
    return lax.dot_general(a, b, (((contract[0],), (contract[1],)), ((), ())), preferred_element_type=F32)


def mm3(a, b):
    return mm(a[0], b[0]) + (mm(a[0], b[1]) + mm(a[1], b[0]))


def params(mib):
    return pltpu.CompilerParams(vmem_limit_bytes=mib * 2**20)


def trade(v, pair, shift):
    t = v[(0 - shift) % 4]
    for m in range(1, 4):
        t = jnp.where(pair == m, v[(m - shift) % 4], t)
    return t


def unturn(x, y, sign):
    out = x
    for s in range(1, 4):
        out = jnp.where(y == s, pltpu.roll(x, (sign * 2 * s) % 8, 1), out)
    return out


def place(z, xh, xl, y):
    return z * 16 + ((xh * 2 + xl - y) % 4) * 4 + y


def place_groups():
    order = [None] * 64
    for z in range(4):
        for xh in range(2):
            for xl in range(2):
                for y in range(4):
                    order[place(z, xh, xl, y)] = ((z * 2 + xh) * 2 + xl) * 4 + y
    return [[chip * 2 + core for chip in order] for core in range(2)]


AHEAD = 7


def forward_kernel(pos_ref, f_hbm, r_hbm, own, oth, rh_ref, rl_ref, f_ref, r_ref, fsem, sem):
    def fetch_f(g):
        cut = pl.ds(g * 4, 4)
        return pltpu.make_async_copy(f_hbm.at[cut], f_ref.at[cut], fsem.at[g])

    def fetch(k):
        return pltpu.make_async_copy(r_hbm.at[k], r_ref.at[k], sem.at[k])

    fetch_f(0).start()
    for k in range(AHEAD):
        fetch(k).start()
    for g in range(1, 4):
        fetch_f(g).start()
    core = pos_ref[0]
    row = lax.broadcasted_iota(jnp.int32, (64, 64), 0)
    col = lax.broadcasted_iota(jnp.int32, (64, 64), 1)
    perms = []
    for q in range(4):
        c = (row // 32 + core) % 2
        y = ((row // 2) % 4 + 4 - q) % 4
        src = (row % 2) * 32 + ((row // 8) % 2) * 16 + y * 4 + c * 2 + (row // 16) % 2
        perms.append(jnp.where(col == src, 1.0, 0.0).astype(BF16))
    pair = lax.broadcasted_iota(jnp.int32, (8, 128), 0) // 2

    def operands(g):
        lhs = []
        for q in range(4):
            fr, fi = f_ref[g * 4 + q, 0], f_ref[g * 4 + q, 1]
            x = jnp.concatenate(
                [jnp.concatenate([fr, -fi], axis=1), jnp.concatenate([fi, fr], axis=1)], axis=0
            )
            xh, xl = split(x)
            ph, plo = mm(perms[q], xh).astype(BF16), mm(perms[q], xl).astype(BF16)
            lhs.append((ph, jnp.concatenate([ph, plo], axis=0)))
        return lhs

    def block(g, g8, z, lhs):
        rows = slice(z * 256, (z + 1) * 256)
        res = []
        for q in range(4):
            k = g * 4 + q
            wh, wl = split(jnp.concatenate([r_ref[k, 0, rows, :], r_ref[k, 1, rows, :]], axis=1))
            rh_ref[k, rows, :] = wh
            rl_ref[k, rows, :] = wl
            if q % 2:
                low = jnp.concatenate([lhs[q][0], jnp.zeros_like(lhs[q][0])], axis=0)
                acc = (mm(wh, lhs[q][1], (1, 1)) + mm(wl, low, (1, 1))).T
                res.append(acc[:64] + acc[64:])
            else:
                acc = mm(lhs[q][1], wh, (1, 1))
                res.append(acc[:64] + (acc[64:] + mm(lhs[q][0], wl, (1, 1))))
        for xh_ in range(2):
            for part in range(8):
                v = [r[part * 8 : part * 8 + 8, xh_ * 128 : xh_ * 128 + 128] for r in res]
                out = oth if part // 4 else own
                for y in range(4):
                    out[place(z, xh_, part % 2, y), (part // 2) % 2, g8, :] = trade(v, pair, y)

    @pl.loop(0, 4)
    def _(g):
        fetch_f(g).wait()
        lhs = operands(g)
        g8 = pl.ds(pl.multiple_of(g * 8, 8), 8)
        for q in range(4):
            k = g * 4 + q
            fetch(k).wait()

            @pl.when(k + AHEAD < KK)
            def _():
                fetch(k + AHEAD).start()

        for z in range(4):
            block(g, g8, z, lhs)


def forward_panel(pos, focusing, reflection):
    panel = jax.ShapeDtypeStruct((64, 2, 32, 128), F32)
    half = jax.ShapeDtypeStruct((KK, 1024, 256), BF16)
    return pl.pallas_call(
        forward_kernel,
        in_specs=[SMEM, HBM, HBM],
        out_specs=[VMEM] * 4,
        out_shape=[panel] * 2 + [half] * 2,
        scratch_shapes=[
            pltpu.VMEM((KK, 2, 32, 128), F32),
            pltpu.VMEM((KK, 2, 1024, 128), F32),
            pltpu.SemaphoreType.DMA((4,)),
            pltpu.SemaphoreType.DMA((16,)),
        ],
        compiler_params=params(24),
        cost_estimate=pl.CostEstimate(flops=3 * 2**30, bytes_accessed=21 * 2**20, transcendentals=0),
        name="forward_panel",
    )(pos, focusing, reflection)


def source_kernel(pos_ref, th_ref, tl_ref, tth_ref, ttl_ref, mute_ref, x_ref, time_ref, out_ref):
    turn = pos_ref[2]
    cols = []
    for j in range(2):
        groups = []
        for f in range(KB):
            t = [x_ref[place(f // 2, f % 2, i // 4, i % 4), j] for i in range(8)]
            groups.append(((t[0] + t[1]) + (t[2] + t[3])) + ((t[4] + t[5]) + (t[6] + t[7])))
        x = jnp.concatenate(groups, axis=0)
        cols.append(unturn(x.reshape(32, 8, 128), turn, -1).reshape(256, 128))
    up = mm3((th_ref[...], tl_ref[...]), split(jnp.concatenate(cols, axis=1)))
    t = lax.broadcasted_iota(jnp.int32, (NT, 128), 0)
    kept = []
    for j in range(2):
        mute = jnp.broadcast_to(mute_ref[j : j + 1, :], (NT, 128))
        val = jnp.where((t < mute) | (t > NT - mute), up[:, j * 128 : (j + 1) * 128], 0.0)
        time_ref[pl.ds(j, NT, stride=2), :] = val
        kept.append(val)
    back = mm3((tth_ref[...], ttl_ref[...]), split(jnp.concatenate(kept, axis=1)))
    for j in range(2):
        b = unturn(back[:, j * 128 : (j + 1) * 128].reshape(32, 8, 128), turn, 1)
        b = b.reshape(KB, 32, 128)
        for f in range(KB):
            for i in range(8):
                out_ref[place(f // 2, f % 2, i // 4, i % 4), j] = b[f]


def source_traces(pos, tables, mute, parts):
    return pl.pallas_call(
        source_kernel,
        in_specs=[SMEM] + [VMEM] * 6,
        out_specs=[VMEM] * 2,
        out_shape=[
            jax.ShapeDtypeStruct((NT * 2, 128), F32),
            jax.ShapeDtypeStruct((64, 2, 32, 128), F32),
        ],
        compiler_params=params(8),
        name="source_traces",
    )(pos, *tables, mute, parts)


def adjoint_kernel(second, own, oth, rh_ref, rl_ref, *rest):
    out_ref = rest[-1]
    pair = lax.broadcasted_iota(jnp.int32, (8, 128), 0) // 2
    even = (lax.broadcasted_iota(jnp.int32, (64, 128), 0) % 2) == 0

    for g in range(4):
        g8 = slice(g * 8, g * 8 + 8)
        acc = [None] * 4
        for zz in range(2):
            z = second * 2 + zz
            lhs = [[None] * 2 for _ in range(4)]
            for xh_ in range(2):
                tiles = [[] for _ in range(4)]
                for part in range(8):
                    j, xlo = part // 4, part % 2
                    if (part // 2) % 2:
                        v = [oth[place(zz, xh_, xlo, y), j, g8, :] for y in range(4)]
                    else:
                        v = [own[place(z, xh_, xlo, y), j, g8, :] for y in range(4)]
                    for q in range(4):
                        tiles[q].append(trade(v, pair, q))
                for q in range(4):
                    lhs[q][xh_] = jnp.concatenate(tiles[q], axis=0)
            rows = slice(z * 256, (z + 1) * 256)
            for q in range(4):
                bh, bl = split(jnp.concatenate(lhs[q], axis=1))
                wh, wl = rh_ref[g * 4 + q, rows, :], rl_ref[g * 4 + q, rows, :]
                both = mm(jnp.concatenate([bh, bl], axis=0), wh)
                add = both[:64] + (both[64:] + mm(bh, wl))
                acc[q] = add if acc[q] is None else acc[q] + add
        res = []
        for q in range(4):
            a, b = acc[q][:, :128], acc[q][:, 128:]
            res.append(a + jnp.where(even, pltpu.roll(b, 63, 0), -pltpu.roll(b, 1, 0)))
        for part in range(8):
            v = [r[part * 8 : part * 8 + 8] for r in res]
            for y in range(4):
                at = ((part % 2) * 4 + y, part // 2, g8, slice(None))
                t = trade(v, pair, y)
                out_ref[at] = rest[0][at] + t if second else t


def adjoint_panel(second, own, oth, rh, rl, *before):
    return pl.pallas_call(
        functools.partial(adjoint_kernel, second),
        in_specs=[VMEM] * (4 + len(before)),
        out_specs=VMEM,
        out_shape=jax.ShapeDtypeStruct((8, 4, 32, 128), F32),
        compiler_params=params(8),
        cost_estimate=pl.CostEstimate(flops=3 * 2**29, bytes_accessed=2**20, transcendentals=0),
        name=f"adjoint_panel{second}",
    )(own, oth, rh, rl, *before)


def receiver_kernel(
    pos_ref, th_ref, tl_ref, mute_ref, direct_ref, x_ref, time_ref, out_ref, time_hbm, sem
):
    copy = pltpu.make_async_copy(time_ref, time_hbm, sem)
    copy.start()
    even = pos_ref[0] == 0
    turn = pos_ref[1]
    t = lax.broadcasted_iota(jnp.int32, (NT, 128), 0)
    for c in range(2):
        cols = []
        for j in range(2):
            a = jnp.where(even, x_ref[:, j * 2 + c], x_ref[:, j * 2 + 1 - c])
            cols.append(unturn(a.reshape(32, 8, 128), turn, -1).reshape(256, 128))
        adj = mm3((th_ref[...], tl_ref[...]), split(jnp.concatenate(cols, axis=1)))
        for j in range(2):
            p = c * 2 + j
            mute = jnp.broadcast_to(mute_ref[p : p + 1, :], (NT, 128))
            val = jnp.where((t < mute) | (t > NT - mute), adj[:, j * 128 : (j + 1) * 128], 0.0)
            rows = pl.ds(p, NT, stride=4)
            out_ref[rows, :] = direct_ref[rows, :] - val
    copy.wait()


def receiver_traces(pos, tables, mute, direct, x, time):
    return pl.pallas_call(
        receiver_kernel,
        in_specs=[SMEM] + [VMEM] * 6,
        out_specs=[VMEM, HBM],
        out_shape=[
            jax.ShapeDtypeStruct((NT * 4, 128), F32),
            jax.ShapeDtypeStruct((NT * 2, 128), F32),
        ],
        scratch_shapes=[pltpu.SemaphoreType.DMA],
        compiler_params=params(8),
        name="receiver_traces",
    )(pos, *tables, mute, direct, x, time)


SWAP = [(0, 1), (1, 0)]
EVERY = ("z", "xh", "xl", "y", "c")


def exchange(x):
    return lax.all_to_all(
        x, EVERY, split_axis=0, concat_axis=0, tiled=True, axis_index_groups=place_groups()
    )


def body(reflection, focusing, direct_wave, mute_source, mute_receiver):
    core, z, y = lax.axis_index("c"), lax.axis_index("z"), lax.axis_index("y")
    pos = jnp.stack([core, (z & 1) * 2 + lax.axis_index("xh"), y])
    table = dft_table()
    th, tl = split_const(table)

    focusing = pltpu.with_memory_space_constraint(focusing, pltpu.HBM)
    reflection = pltpu.with_memory_space_constraint(reflection, pltpu.HBM)
    own, oth, rh, rl = forward_panel(pos, focusing, reflection)
    parts = exchange(own + lax.ppermute(oth, "c", SWAP))
    time, back = source_traces(pos, (th, tl, th.T, tl.T), mute_source, parts)
    b_own = exchange(back)
    b_oth = [lax.ppermute(b_own[i * 32 : i * 32 + 32], "c", SWAP) for i in range(2)]
    adjoint = adjoint_panel(0, b_own, b_oth[0], rh, rl)
    adjoint = adjoint_panel(1, b_own, b_oth[1], rh, rl, adjoint)
    received = lax.all_to_all(adjoint, ("z", "xh"), split_axis=0, concat_axis=0, tiled=True)
    plus, time = receiver_traces(
        pos, (th, tl), mute_receiver, direct_wave.reshape(NT * 4, 128), received, time
    )
    return time.reshape(NT, 2, 128), plus.reshape(NT, 4, 128)


def solution(mesh):
    fine = Mesh(mesh.devices.reshape(4, 2, 2, 4, 2), ("z", "xh", "xl", "y", "c"))
    freq, rcv = ("z", "xh"), ("xl", "y", "c")
    return jax.shard_map(
        body,
        mesh=fine,
        in_specs=(
            P(freq, None, None, rcv),
            P(freq, None, None, rcv),
            P(None, freq, rcv),
            P(rcv, freq),
            P(freq, rcv),
        ),
        out_specs=(P(None, rcv, freq), P(None, freq, rcv)),
        check_vma=False,
    )
```

```python
import functools
import math

import numpy as np
import jax
import jax.numpy as jnp
from jax import lax
from jax.experimental import pallas as pl
from jax.experimental.pallas import tpu as pltpu
from jax.sharding import Mesh, PartitionSpec as P

F32, BF16 = jnp.float32, jnp.bfloat16
NT = 256
KB, KK = 8, 16
VMEM = pl.BlockSpec(memory_space=pltpu.VMEM)
SMEM = pl.BlockSpec(memory_space=pltpu.SMEM)
HBM = pl.BlockSpec(memory_space=pltpu.HBM)


def dft_table():
    k = np.arange(1, KB * KK + 1)[None, :]
    t = np.arange(NT)[:, None]
    phase = 2.0 * math.pi * ((k * t) % NT) / NT
    c = 1.0 / math.sqrt(KB * KK)
    return np.stack([c * np.cos(phase), -c * np.sin(phase)], axis=2).reshape(NT, NT)


def split_const(table):
    high = table.astype(np.float32).astype(jnp.bfloat16)
    low = (table - high.astype(np.float64)).astype(np.float32).astype(jnp.bfloat16)
    return np.asarray(high), np.asarray(low)


def split(x):
    high = x.astype(BF16)
    return high, (x - high.astype(F32)).astype(BF16)


def mm(a, b, contract=(1, 0)):
    return lax.dot_general(a, b, (((contract[0],), (contract[1],)), ((), ())), preferred_element_type=F32)


def mm3(a, b):
    return mm(a[0], b[0]) + (mm(a[0], b[1]) + mm(a[1], b[0]))


def params(mib):
    return pltpu.CompilerParams(vmem_limit_bytes=mib * 2**20)


def trade(v, pair, shift):
    t = v[(0 - shift) % 4]
    for m in range(1, 4):
        t = jnp.where(pair == m, v[(m - shift) % 4], t)
    return t


def unturn(x, y, sign):
    out = x
    for s in range(1, 4):
        out = jnp.where(y == s, pltpu.roll(x, (sign * 2 * s) % 8, 1), out)
    return out


def place(z, xh, xl, y):
    return ((z * 2 + xl) * 2 + xh) * 4 + y


AHEAD = 7


def forward_kernel(pos_ref, f_hbm, r_hbm, own, oth, rh_ref, rl_ref, f_ref, r_ref, fsem, sem):
    def fetch_f(g):
        cut = pl.ds(g * 4, 4)
        return pltpu.make_async_copy(f_hbm.at[cut], f_ref.at[cut], fsem.at[g])

    def fetch(k):
        return pltpu.make_async_copy(r_hbm.at[k], r_ref.at[k], sem.at[k])

    fetch_f(0).start()
    for k in range(AHEAD):
        fetch(k).start()
    for g in range(1, 4):
        fetch_f(g).start()
    core = pos_ref[0]
    row = lax.broadcasted_iota(jnp.int32, (64, 64), 0)
    col = lax.broadcasted_iota(jnp.int32, (64, 64), 1)
    perms = []
    for q in range(4):
        c = (row // 32 + core) % 2
        y = ((row // 2) % 4 + 4 - q) % 4
        src = (row % 2) * 32 + ((row // 8) % 2) * 16 + y * 4 + c * 2 + (row // 16) % 2
        perms.append(jnp.where(col == src, 1.0, 0.0).astype(BF16))
    pair = lax.broadcasted_iota(jnp.int32, (8, 128), 0) // 2

    def operands(g):
        lhs = []
        for q in range(4):
            fr, fi = f_ref[g * 4 + q, 0], f_ref[g * 4 + q, 1]
            x = jnp.concatenate(
                [jnp.concatenate([fr, -fi], axis=1), jnp.concatenate([fi, fr], axis=1)], axis=0
            )
            xh, xl = split(x)
            ph, plo = mm(perms[q], xh).astype(BF16), mm(perms[q], xl).astype(BF16)
            lhs.append((ph, jnp.concatenate([ph, plo], axis=0)))
        return lhs

    def block(g, g8, z, lhs):
        rows = slice(z * 256, (z + 1) * 256)
        res = []
        for q in range(4):
            k = g * 4 + q
            wh, wl = split(jnp.concatenate([r_ref[k, 0, rows, :], r_ref[k, 1, rows, :]], axis=1))
            rh_ref[k, rows, :] = wh
            rl_ref[k, rows, :] = wl
            if q % 2:
                low = jnp.concatenate([lhs[q][0], jnp.zeros_like(lhs[q][0])], axis=0)
                acc = (mm(wh, lhs[q][1], (1, 1)) + mm(wl, low, (1, 1))).T
                res.append(acc[:64] + acc[64:])
            else:
                acc = mm(lhs[q][1], wh, (1, 1))
                res.append(acc[:64] + (acc[64:] + mm(lhs[q][0], wl, (1, 1))))
        for xh_ in range(2):
            for part in range(8):
                v = [r[part * 8 : part * 8 + 8, xh_ * 128 : xh_ * 128 + 128] for r in res]
                out = oth if part // 4 else own
                for y in range(4):
                    out[place(z, xh_, part % 2, y), (part // 2) % 2, g8, :] = trade(v, pair, y)

    @pl.loop(0, 4)
    def _(g):
        fetch_f(g).wait()
        lhs = operands(g)
        g8 = pl.ds(pl.multiple_of(g * 8, 8), 8)
        for q in range(4):
            k = g * 4 + q
            fetch(k).wait()

            @pl.when(k + AHEAD < KK)
            def _():
                fetch(k + AHEAD).start()

        for z in range(4):
            block(g, g8, z, lhs)


def forward_panel(pos, focusing, reflection):
    panel = jax.ShapeDtypeStruct((64, 2, 32, 128), F32)
    half = jax.ShapeDtypeStruct((KK, 1024, 256), BF16)
    return pl.pallas_call(
        forward_kernel,
        in_specs=[SMEM, HBM, HBM],
        out_specs=[VMEM] * 4,
        out_shape=[panel] * 2 + [half] * 2,
        scratch_shapes=[
            pltpu.VMEM((KK, 2, 32, 128), F32),
            pltpu.VMEM((KK, 2, 1024, 128), F32),
            pltpu.SemaphoreType.DMA((4,)),
            pltpu.SemaphoreType.DMA((16,)),
        ],
        compiler_params=params(24),
        cost_estimate=pl.CostEstimate(flops=3 * 2**30, bytes_accessed=21 * 2**20, transcendentals=0),
        name="forward_panel",
    )(pos, focusing, reflection)


def source_kernel(pos_ref, th_ref, tl_ref, tth_ref, ttl_ref, mute_ref, x_ref, time_ref, out_ref):
    turn = pos_ref[2]
    cols = []
    for j in range(2):
        groups = []
        for f in range(KB):
            t = [x_ref[place(f // 2, f % 2, i // 4, i % 4), j] for i in range(8)]
            groups.append(((t[0] + t[1]) + (t[2] + t[3])) + ((t[4] + t[5]) + (t[6] + t[7])))
        x = jnp.concatenate(groups, axis=0)
        cols.append(unturn(x.reshape(32, 8, 128), turn, -1).reshape(256, 128))
    up = mm3((th_ref[...], tl_ref[...]), split(jnp.concatenate(cols, axis=1)))
    t = lax.broadcasted_iota(jnp.int32, (NT, 128), 0)
    kept = []
    for j in range(2):
        mute = jnp.broadcast_to(mute_ref[j : j + 1, :], (NT, 128))
        val = jnp.where((t < mute) | (t > NT - mute), up[:, j * 128 : (j + 1) * 128], 0.0)
        time_ref[pl.ds(j, NT, stride=2), :] = val
        kept.append(val)
    back = mm3((tth_ref[...], ttl_ref[...]), split(jnp.concatenate(kept, axis=1)))
    for j in range(2):
        b = unturn(back[:, j * 128 : (j + 1) * 128].reshape(32, 8, 128), turn, 1)
        b = b.reshape(KB, 32, 128)
        for f in range(KB):
            for i in range(8):
                out_ref[place(f // 2, f % 2, i // 4, i % 4), j] = b[f]


def source_traces(pos, tables, mute, parts):
    return pl.pallas_call(
        source_kernel,
        in_specs=[SMEM] + [VMEM] * 6,
        out_specs=[VMEM] * 2,
        out_shape=[
            jax.ShapeDtypeStruct((NT * 2, 128), F32),
            jax.ShapeDtypeStruct((64, 2, 32, 128), F32),
        ],
        compiler_params=params(8),
        name="source_traces",
    )(pos, *tables, mute, parts)


def adjoint_kernel(second, own, oth, rh_ref, rl_ref, extra_ref, out_ref, time_hbm=None, sem=None):
    if not second:
        copy = pltpu.make_async_copy(extra_ref, time_hbm, sem)
        copy.start()
    pair = lax.broadcasted_iota(jnp.int32, (8, 128), 0) // 2
    even = (lax.broadcasted_iota(jnp.int32, (64, 128), 0) % 2) == 0

    for g in range(4):
        g8 = slice(g * 8, g * 8 + 8)
        acc = [None] * 4
        for zz in range(2):
            z = second * 2 + zz
            lhs = [[None] * 2 for _ in range(4)]
            for xh_ in range(2):
                tiles = [[] for _ in range(4)]
                for part in range(8):
                    j, xlo = part // 4, part % 2
                    if (part // 2) % 2:
                        v = [oth[place(zz, xh_, xlo, y), j, g8, :] for y in range(4)]
                    else:
                        v = [own[place(z, xh_, xlo, y), j, g8, :] for y in range(4)]
                    for q in range(4):
                        tiles[q].append(trade(v, pair, q))
                for q in range(4):
                    lhs[q][xh_] = jnp.concatenate(tiles[q], axis=0)
            rows = slice(z * 256, (z + 1) * 256)
            for q in range(4):
                bh, bl = split(jnp.concatenate(lhs[q], axis=1))
                wh, wl = rh_ref[g * 4 + q, rows, :], rl_ref[g * 4 + q, rows, :]
                both = mm(jnp.concatenate([bh, bl], axis=0), wh)
                add = both[:64] + (both[64:] + mm(bh, wl))
                acc[q] = add if acc[q] is None else acc[q] + add
        res = []
        for q in range(4):
            a, b = acc[q][:, :128], acc[q][:, 128:]
            res.append(a + jnp.where(even, pltpu.roll(b, 63, 0), -pltpu.roll(b, 1, 0)))
        for part in range(8):
            v = [r[part * 8 : part * 8 + 8] for r in res]
            for y in range(4):
                at = ((part % 2) * 4 + y, part // 2, g8, slice(None))
                t = trade(v, pair, y)
                out_ref[at] = extra_ref[at] + t if second else t
    if not second:
        copy.wait()


def adjoint_panel(second, own, oth, rh, rl, extra):
    panel = jax.ShapeDtypeStruct((8, 4, 32, 128), F32)
    time = jax.ShapeDtypeStruct((NT * 2, 128), F32)
    return pl.pallas_call(
        functools.partial(adjoint_kernel, second),
        in_specs=[VMEM] * 5,
        out_specs=VMEM if second else [VMEM, HBM],
        out_shape=panel if second else [panel, time],
        scratch_shapes=[] if second else [pltpu.SemaphoreType.DMA],
        compiler_params=params(8),
        cost_estimate=pl.CostEstimate(flops=3 * 2**29, bytes_accessed=2**20, transcendentals=0),
        name=f"adjoint_panel{second}",
    )(own, oth, rh, rl, extra)


def receiver_kernel(pos_ref, th_ref, tl_ref, mute_ref, direct_ref, x_ref, out_ref):
    even = pos_ref[0] == 0
    turn = pos_ref[1]
    t = lax.broadcasted_iota(jnp.int32, (NT, 128), 0)
    for c in range(2):
        cols = []
        for j in range(2):
            a = jnp.where(even, x_ref[:, j * 2 + c], x_ref[:, j * 2 + 1 - c])
            cols.append(unturn(a.reshape(32, 8, 128), turn, -1).reshape(256, 128))
        adj = mm3((th_ref[...], tl_ref[...]), split(jnp.concatenate(cols, axis=1)))
        for j in range(2):
            p = c * 2 + j
            mute = jnp.broadcast_to(mute_ref[p : p + 1, :], (NT, 128))
            val = jnp.where((t < mute) | (t > NT - mute), adj[:, j * 128 : (j + 1) * 128], 0.0)
            rows = pl.ds(p, NT, stride=4)
            out_ref[rows, :] = direct_ref[rows, :] - val


def receiver_traces(pos, tables, mute, direct, x):
    return pl.pallas_call(
        receiver_kernel,
        in_specs=[SMEM] + [VMEM] * 5,
        out_specs=VMEM,
        out_shape=jax.ShapeDtypeStruct((NT * 4, 128), F32),
        compiler_params=params(8),
        name="receiver_traces",
    )(pos, *tables, mute, direct, x)


SWAP = [(0, 1), (1, 0)]
CHIPS = ("z", "xl", "xh", "y")


def exchange(x, axes):
    return lax.all_to_all(x, axes, split_axis=0, concat_axis=0, tiled=True)


def body(reflection, focusing, direct_wave, mute_source, mute_receiver):
    core, z, y = lax.axis_index("c"), lax.axis_index("z"), lax.axis_index("y")
    pos = jnp.stack([core, (z & 1) * 2 + lax.axis_index("xh"), y])
    table = dft_table()
    th, tl = split_const(table)

    focusing = pltpu.with_memory_space_constraint(focusing, pltpu.HBM)
    reflection = pltpu.with_memory_space_constraint(reflection, pltpu.HBM)
    own, oth, rh, rl = forward_panel(pos, focusing, reflection)
    parts = exchange(own + lax.ppermute(oth, "c", SWAP), CHIPS)
    time, back = source_traces(pos, (th, tl, th.T, tl.T), mute_source, parts)
    b_own = exchange(back, CHIPS)
    b_oth = [lax.ppermute(b_own[i * 32 : i * 32 + 32], "c", SWAP) for i in range(2)]
    adjoint, time = adjoint_panel(0, b_own, b_oth[0], rh, rl, time)
    adjoint = adjoint_panel(1, b_own, b_oth[1], rh, rl, adjoint)
    received = exchange(adjoint, ("z", "xh"))
    plus = receiver_traces(
        pos, (th, tl), mute_receiver, direct_wave.reshape(NT * 4, 128), received
    )
    return time.reshape(NT, 2, 128), plus.reshape(NT, 4, 128)


def solution(mesh):
    fine = Mesh(mesh.devices.reshape(4, 2, 2, 4, 2), ("z", "xh", "xl", "y", "c"))
    freq, rcv = ("z", "xh"), ("xl", "y", "c")
    return jax.shard_map(
        body,
        mesh=fine,
        in_specs=(
            P(freq, None, None, rcv),
            P(freq, None, None, rcv),
            P(None, freq, rcv),
            P(rcv, freq),
            P(freq, rcv),
        ),
        out_specs=(P(None, rcv, freq), P(None, freq, rcv)),
        check_vma=False,
    )
```

```python
import functools
import math

import numpy as np
import jax
import jax.numpy as jnp
from jax import lax
from jax.experimental import pallas as pl
from jax.experimental.pallas import tpu as pltpu
from jax.sharding import Mesh, PartitionSpec as P

F32, BF16 = jnp.float32, jnp.bfloat16
NT = 256
KB, KK = 8, 16
VMEM = pl.BlockSpec(memory_space=pltpu.VMEM)
SMEM = pl.BlockSpec(memory_space=pltpu.SMEM)
HBM = pl.BlockSpec(memory_space=pltpu.HBM)


def dft_table():
    k = np.arange(1, KB * KK + 1)[None, :]
    t = np.arange(NT)[:, None]
    phase = 2.0 * math.pi * ((k * t) % NT) / NT
    c = 1.0 / math.sqrt(KB * KK)
    return np.stack([c * np.cos(phase), -c * np.sin(phase)], axis=2).reshape(NT, NT)


def split_const(table):
    high = table.astype(np.float32).astype(jnp.bfloat16)
    low = (table - high.astype(np.float64)).astype(np.float32).astype(jnp.bfloat16)
    return np.asarray(high), np.asarray(low)


def split(x):
    high = x.astype(BF16)
    return high, (x - high.astype(F32)).astype(BF16)


def mm(a, b, contract=(1, 0)):
    return lax.dot_general(a, b, (((contract[0],), (contract[1],)), ((), ())), preferred_element_type=F32)


def mm3(a, b):
    return mm(a[0], b[0]) + (mm(a[0], b[1]) + mm(a[1], b[0]))


def params(mib):
    return pltpu.CompilerParams(vmem_limit_bytes=mib * 2**20)


def trade(v, pair, shift):
    t = v[(0 - shift) % 4]
    for m in range(1, 4):
        t = jnp.where(pair == m, v[(m - shift) % 4], t)
    return t


def unturn(x, y, sign):
    out = x
    for s in range(1, 4):
        out = jnp.where(y == s, pltpu.roll(x, (sign * 2 * s) % 8, 1), out)
    return out


def place(z, xh, xl, y):
    return ((xh * 4 + z) * 2 + xl) * 4 + y


AHEAD = 7


def forward_kernel(pos_ref, f_hbm, r_hbm, own, oth, rh_ref, rl_ref, f_ref, r_ref, fsem, sem):
    def fetch_f(g):
        cut = pl.ds(g * 4, 4)
        return pltpu.make_async_copy(f_hbm.at[cut], f_ref.at[cut], fsem.at[g])

    def fetch(k):
        return pltpu.make_async_copy(r_hbm.at[k], r_ref.at[k], sem.at[k])

    fetch_f(0).start()
    for k in range(AHEAD):
        fetch(k).start()
    for g in range(1, 4):
        fetch_f(g).start()
    core = pos_ref[0]
    row = lax.broadcasted_iota(jnp.int32, (64, 64), 0)
    col = lax.broadcasted_iota(jnp.int32, (64, 64), 1)
    perms = []
    for q in range(4):
        c = (row // 32 + core) % 2
        y = ((row // 2) % 4 + 4 - q) % 4
        src = (row % 2) * 32 + ((row // 8) % 2) * 16 + y * 4 + c * 2 + (row // 16) % 2
        perms.append(jnp.where(col == src, 1.0, 0.0).astype(BF16))
    pair = lax.broadcasted_iota(jnp.int32, (8, 128), 0) // 2

    def operands(g):
        lhs = []
        for q in range(4):
            fr, fi = f_ref[g * 4 + q, 0], f_ref[g * 4 + q, 1]
            x = jnp.concatenate(
                [jnp.concatenate([fr, -fi], axis=1), jnp.concatenate([fi, fr], axis=1)], axis=0
            )
            xh, xl = split(x)
            ph, plo = mm(perms[q], xh).astype(BF16), mm(perms[q], xl).astype(BF16)
            lhs.append((ph, jnp.concatenate([ph, plo], axis=0)))
        return lhs

    def block(g, g8, z, lhs):
        rows = slice(z * 256, (z + 1) * 256)
        res = []
        for q in range(4):
            k = g * 4 + q
            wh, wl = split(jnp.concatenate([r_ref[k, 0, rows, :], r_ref[k, 1, rows, :]], axis=1))
            rh_ref[k, rows, :] = wh
            rl_ref[k, rows, :] = wl
            if q % 2:
                low = jnp.concatenate([lhs[q][0], jnp.zeros_like(lhs[q][0])], axis=0)
                acc = (mm(wh, lhs[q][1], (1, 1)) + mm(wl, low, (1, 1))).T
                res.append(acc[:64] + acc[64:])
            else:
                acc = mm(lhs[q][1], wh, (1, 1))
                res.append(acc[:64] + (acc[64:] + mm(lhs[q][0], wl, (1, 1))))
        for xh_ in range(2):
            for part in range(8):
                v = [r[part * 8 : part * 8 + 8, xh_ * 128 : xh_ * 128 + 128] for r in res]
                out = oth if part // 4 else own
                for y in range(4):
                    out[place(z, xh_, part % 2, y), (part // 2) % 2, g8, :] = trade(v, pair, y)

    @pl.loop(0, 4)
    def _(g):
        fetch_f(g).wait()
        lhs = operands(g)
        g8 = pl.ds(pl.multiple_of(g * 8, 8), 8)
        for q in range(4):
            k = g * 4 + q
            fetch(k).wait()

            @pl.when(k + AHEAD < KK)
            def _():
                fetch(k + AHEAD).start()

        for z in range(4):
            block(g, g8, z, lhs)


def forward_panel(pos, focusing, reflection):
    panel = jax.ShapeDtypeStruct((64, 2, 32, 128), F32)
    half = jax.ShapeDtypeStruct((KK, 1024, 256), BF16)
    return pl.pallas_call(
        forward_kernel,
        in_specs=[SMEM, HBM, HBM],
        out_specs=[VMEM] * 4,
        out_shape=[panel] * 2 + [half] * 2,
        scratch_shapes=[
            pltpu.VMEM((KK, 2, 32, 128), F32),
            pltpu.VMEM((KK, 2, 1024, 128), F32),
            pltpu.SemaphoreType.DMA((4,)),
            pltpu.SemaphoreType.DMA((16,)),
        ],
        compiler_params=params(24),
        cost_estimate=pl.CostEstimate(flops=3 * 2**30, bytes_accessed=21 * 2**20, transcendentals=0),
        name="forward_panel",
    )(pos, focusing, reflection)


def source_kernel(pos_ref, th_ref, tl_ref, tth_ref, ttl_ref, mute_ref, x_ref, time_ref, out_ref):
    turn = pos_ref[2]
    cols = []
    for j in range(2):
        groups = []
        for f in range(KB):
            t = [x_ref[place(f // 2, f % 2, i // 4, i % 4), j] for i in range(8)]
            groups.append(((t[0] + t[1]) + (t[2] + t[3])) + ((t[4] + t[5]) + (t[6] + t[7])))
        x = jnp.concatenate(groups, axis=0)
        cols.append(unturn(x.reshape(32, 8, 128), turn, -1).reshape(256, 128))
    up = mm3((th_ref[...], tl_ref[...]), split(jnp.concatenate(cols, axis=1)))
    t = lax.broadcasted_iota(jnp.int32, (NT, 128), 0)
    kept = []
    for j in range(2):
        mute = jnp.broadcast_to(mute_ref[j : j + 1, :], (NT, 128))
        val = jnp.where((t < mute) | (t > NT - mute), up[:, j * 128 : (j + 1) * 128], 0.0)
        time_ref[pl.ds(j, NT, stride=2), :] = val
        kept.append(val)
    back = mm3((tth_ref[...], ttl_ref[...]), split(jnp.concatenate(kept, axis=1)))
    for j in range(2):
        b = unturn(back[:, j * 128 : (j + 1) * 128].reshape(32, 8, 128), turn, 1)
        b = b.reshape(KB, 32, 128)
        for f in range(KB):
            for i in range(8):
                out_ref[place(f // 2, f % 2, i // 4, i % 4), j] = b[f]


def source_traces(pos, tables, mute, parts):
    return pl.pallas_call(
        source_kernel,
        in_specs=[SMEM] + [VMEM] * 6,
        out_specs=[VMEM] * 2,
        out_shape=[
            jax.ShapeDtypeStruct((NT * 2, 128), F32),
            jax.ShapeDtypeStruct((64, 2, 32, 128), F32),
        ],
        compiler_params=params(8),
        name="source_traces",
    )(pos, *tables, mute, parts)


def adjoint_kernel(second, own, oth, rh_ref, rl_ref, extra_ref, out_ref, time_hbm=None, sem=None):
    if not second:
        copy = pltpu.make_async_copy(extra_ref, time_hbm, sem)
        copy.start()
    pair = lax.broadcasted_iota(jnp.int32, (8, 128), 0) // 2
    even = (lax.broadcasted_iota(jnp.int32, (64, 128), 0) % 2) == 0

    for g in range(4):
        g8 = slice(g * 8, g * 8 + 8)
        acc = [None] * 4
        for zz in range(2):
            z = second * 2 + zz
            lhs = [[None] * 2 for _ in range(4)]
            for xh_ in range(2):
                tiles = [[] for _ in range(4)]
                for part in range(8):
                    j, xlo = part // 4, part % 2
                    if (part // 2) % 2:
                        v = [oth[((xh_ * 2 + zz) * 2 + xlo) * 4 + y, j, g8, :] for y in range(4)]
                    else:
                        v = [own[place(z, xh_, xlo, y), j, g8, :] for y in range(4)]
                    for q in range(4):
                        tiles[q].append(trade(v, pair, q))
                for q in range(4):
                    lhs[q][xh_] = jnp.concatenate(tiles[q], axis=0)
            rows = slice(z * 256, (z + 1) * 256)
            for q in range(4):
                bh, bl = split(jnp.concatenate(lhs[q], axis=1))
                wh, wl = rh_ref[g * 4 + q, rows, :], rl_ref[g * 4 + q, rows, :]
                both = mm(jnp.concatenate([bh, bl], axis=0), wh)
                add = both[:64] + (both[64:] + mm(bh, wl))
                acc[q] = add if acc[q] is None else acc[q] + add
        res = []
        for q in range(4):
            a, b = acc[q][:, :128], acc[q][:, 128:]
            res.append(a + jnp.where(even, pltpu.roll(b, 63, 0), -pltpu.roll(b, 1, 0)))
        for part in range(8):
            v = [r[part * 8 : part * 8 + 8] for r in res]
            for y in range(4):
                at = ((part % 2) * 4 + y, part // 2, g8, slice(None))
                t = trade(v, pair, y)
                out_ref[at] = extra_ref[at] + t if second else t
    if not second:
        copy.wait()


def adjoint_panel(second, own, oth, rh, rl, extra):
    panel = jax.ShapeDtypeStruct((8, 4, 32, 128), F32)
    time = jax.ShapeDtypeStruct((NT * 2, 128), F32)
    return pl.pallas_call(
        functools.partial(adjoint_kernel, second),
        in_specs=[VMEM] * 5,
        out_specs=VMEM if second else [VMEM, HBM],
        out_shape=panel if second else [panel, time],
        scratch_shapes=[] if second else [pltpu.SemaphoreType.DMA],
        compiler_params=params(8),
        cost_estimate=pl.CostEstimate(flops=3 * 2**29, bytes_accessed=2**20, transcendentals=0),
        name=f"adjoint_panel{second}",
    )(own, oth, rh, rl, extra)


def receiver_kernel(pos_ref, th_ref, tl_ref, mute_ref, direct_ref, x_ref, out_hbm, out_ref, sem):
    even = pos_ref[0] == 0
    turn = pos_ref[1]
    adj = []
    for c in range(2):
        cols = []
        for j in range(2):
            a = jnp.where(even, x_ref[:, j * 2 + c], x_ref[:, j * 2 + 1 - c])
            cols.append(unturn(a.reshape(32, 8, 128), turn, -1).reshape(256, 128))
        adj.append(mm3((th_ref[...], tl_ref[...]), split(jnp.concatenate(cols, axis=1))))
    copies = []
    for b in range(4):
        t = lax.broadcasted_iota(jnp.int32, (64, 128), 0) + b * 64
        for p in range(4):
            mute = jnp.broadcast_to(mute_ref[p : p + 1, :], (64, 128))
            val = adj[p // 2][b * 64 : b * 64 + 64, (p % 2) * 128 : (p % 2) * 128 + 128]
            rows = pl.ds(b * 256 + p, 64, stride=4)
            kept = jnp.where((t < mute) | (t > NT - mute), val, 0.0)
            out_ref[rows, :] = direct_ref[rows, :] - kept
        cut = pl.ds(b * 256, 256)
        copies.append(pltpu.make_async_copy(out_ref.at[cut], out_hbm.at[cut], sem.at[b]))
        copies[b].start()
    for copy in copies:
        copy.wait()


def receiver_traces(pos, tables, mute, direct, x):
    return pl.pallas_call(
        receiver_kernel,
        in_specs=[SMEM] + [VMEM] * 5,
        out_specs=HBM,
        out_shape=jax.ShapeDtypeStruct((NT * 4, 128), F32),
        scratch_shapes=[pltpu.VMEM((NT * 4, 128), F32), pltpu.SemaphoreType.DMA((4,))],
        compiler_params=params(8),
        name="receiver_traces",
    )(pos, *tables, mute, direct, x)


SWAP = [(0, 1), (1, 0)]
CHIPS = ("xh", "z", "xl", "y")


def exchange(x, axes):
    return lax.all_to_all(x, axes, split_axis=0, concat_axis=0, tiled=True)


def body(reflection, focusing, direct_wave, mute_source, mute_receiver):
    core, z, y = lax.axis_index("c"), lax.axis_index("z"), lax.axis_index("y")
    pos = jnp.stack([core, (z & 1) * 2 + lax.axis_index("xh"), y])
    table = dft_table()
    th, tl = split_const(table)

    focusing = pltpu.with_memory_space_constraint(focusing, pltpu.HBM)
    reflection = pltpu.with_memory_space_constraint(reflection, pltpu.HBM)
    own, oth, rh, rl = forward_panel(pos, focusing, reflection)
    parts = exchange(own + lax.ppermute(oth, "c", SWAP), CHIPS)
    time, back = source_traces(pos, (th, tl, th.T, tl.T), mute_source, parts)
    b_own = exchange(back, CHIPS)
    by_z = b_own.reshape(2, 4, 8, 2, 32, 128)
    b_oth = [
        lax.ppermute(by_z[:, i * 2 : i * 2 + 2].reshape(32, 2, 32, 128), "c", SWAP) for i in range(2)
    ]
    adjoint, time = adjoint_panel(0, b_own, b_oth[0], rh, rl, time)
    adjoint = adjoint_panel(1, b_own, b_oth[1], rh, rl, adjoint)
    received = exchange(adjoint, ("z", "xh"))
    plus = receiver_traces(
        pos, (th, tl), mute_receiver, direct_wave.reshape(NT * 4, 128), received
    )
    return time.reshape(NT, 2, 128), plus.reshape(NT, 4, 128)


def solution(mesh):
    fine = Mesh(mesh.devices.reshape(4, 2, 2, 4, 2), ("z", "xh", "xl", "y", "c"))
    freq, rcv = ("z", "xh"), ("xl", "y", "c")
    return jax.shard_map(
        body,
        mesh=fine,
        in_specs=(
            P(freq, None, None, rcv),
            P(freq, None, None, rcv),
            P(None, freq, rcv),
            P(rcv, freq),
            P(freq, rcv),
        ),
        out_specs=(P(None, rcv, freq), P(None, freq, rcv)),
        check_vma=False,
    )
```

```python
import functools
import math

import numpy as np
import jax
import jax.numpy as jnp
from jax import lax
from jax.experimental import pallas as pl
from jax.experimental.pallas import tpu as pltpu
from jax.sharding import Mesh, PartitionSpec as P

F32, BF16 = jnp.float32, jnp.bfloat16
NT = 256
KB, KK = 8, 16
VMEM = pl.BlockSpec(memory_space=pltpu.VMEM)
SMEM = pl.BlockSpec(memory_space=pltpu.SMEM)
HBM = pl.BlockSpec(memory_space=pltpu.HBM)


def dft_table():
    k = np.arange(1, KB * KK + 1)[None, :]
    t = np.arange(NT)[:, None]
    phase = 2.0 * math.pi * ((k * t) % NT) / NT
    c = 1.0 / math.sqrt(KB * KK)
    return np.stack([c * np.cos(phase), -c * np.sin(phase)], axis=2).reshape(NT, NT)


def split_const(table):
    high = table.astype(np.float32).astype(jnp.bfloat16)
    low = (table - high.astype(np.float64)).astype(np.float32).astype(jnp.bfloat16)
    return np.asarray(high), np.asarray(low)


def split(x):
    high = x.astype(BF16)
    return high, (x - high.astype(F32)).astype(BF16)


def mm(a, b, contract=(1, 0)):
    return lax.dot_general(a, b, (((contract[0],), (contract[1],)), ((), ())), preferred_element_type=F32)


def mm3(a, b):
    return mm(
        jnp.concatenate([a[0], a[0], a[1]], axis=1), jnp.concatenate([b[0], b[1], b[0]], axis=0)
    )


def params(mib):
    return pltpu.CompilerParams(vmem_limit_bytes=mib * 2**20)


def trade(v, pair, shift):
    t = v[(0 - shift) % 4]
    for m in range(1, 4):
        t = jnp.where(pair == m, v[(m - shift) % 4], t)
    return t


def unturn(x, y, sign):
    out = x
    for s in range(1, 4):
        out = jnp.where(y == s, pltpu.roll(x, (sign * 2 * s) % 8, 1), out)
    return out


def place(z, xh, xl, y):
    return ((z * 2 + xl) * 2 + xh) * 4 + y


AHEAD = 7


def forward_kernel(pos_ref, f_hbm, r_hbm, own, oth, rh_ref, rl_ref, f_ref, r_ref, fsem, sem):
    def fetch_f(g):
        cut = pl.ds(g * 4, 4)
        return pltpu.make_async_copy(f_hbm.at[cut], f_ref.at[cut], fsem.at[g])

    def fetch(k):
        return pltpu.make_async_copy(r_hbm.at[k], r_ref.at[k], sem.at[k])

    fetch_f(0).start()
    for k in range(AHEAD):
        fetch(k).start()
    for g in range(1, 4):
        fetch_f(g).start()
    core = pos_ref[0]
    row = lax.broadcasted_iota(jnp.int32, (64, 64), 0)
    col = lax.broadcasted_iota(jnp.int32, (64, 64), 1)
    perms = []
    for q in range(4):
        c = (row // 32 + core) % 2
        y = ((row // 2) % 4 + 4 - q) % 4
        src = (row % 2) * 32 + ((row // 8) % 2) * 16 + y * 4 + c * 2 + (row // 16) % 2
        perms.append(jnp.where(col == src, 1.0, 0.0).astype(BF16))
    pair = lax.broadcasted_iota(jnp.int32, (8, 128), 0) // 2

    def operands(g):
        lhs = []
        for q in range(4):
            fr, fi = f_ref[g * 4 + q, 0], f_ref[g * 4 + q, 1]
            x = jnp.concatenate(
                [jnp.concatenate([fr, -fi], axis=1), jnp.concatenate([fi, fr], axis=1)], axis=0
            )
            xh, xl = split(x)
            ph, plo = mm(perms[q], xh).astype(BF16), mm(perms[q], xl).astype(BF16)
            lhs.append((ph, jnp.concatenate([ph, plo], axis=0)))
        return lhs

    def block(g, g8, z, lhs):
        rows = slice(z * 256, (z + 1) * 256)
        res = []
        for q in range(4):
            k = g * 4 + q
            wh, wl = split(jnp.concatenate([r_ref[k, 0, rows, :], r_ref[k, 1, rows, :]], axis=1))
            rh_ref[k, rows, :] = wh
            rl_ref[k, rows, :] = wl
            if q % 2:
                low = jnp.concatenate([lhs[q][0], jnp.zeros_like(lhs[q][0])], axis=0)
                acc = (mm(wh, lhs[q][1], (1, 1)) + mm(wl, low, (1, 1))).T
                res.append(acc[:64] + acc[64:])
            else:
                acc = mm(lhs[q][1], wh, (1, 1))
                res.append(acc[:64] + (acc[64:] + mm(lhs[q][0], wl, (1, 1))))
        for xh_ in range(2):
            for part in range(8):
                v = [r[part * 8 : part * 8 + 8, xh_ * 128 : xh_ * 128 + 128] for r in res]
                out = oth if part // 4 else own
                for y in range(4):
                    out[place(z, xh_, part % 2, y), (part // 2) % 2, g8, :] = trade(v, pair, y)

    @pl.loop(0, 4)
    def _(g):
        fetch_f(g).wait()
        lhs = operands(g)
        g8 = pl.ds(pl.multiple_of(g * 8, 8), 8)
        for q in range(4):
            k = g * 4 + q
            fetch(k).wait()

            @pl.when(k + AHEAD < KK)
            def _():
                fetch(k + AHEAD).start()

        for z in range(4):
            block(g, g8, z, lhs)


def forward_panel(pos, focusing, reflection):
    panel = jax.ShapeDtypeStruct((64, 2, 32, 128), F32)
    half = jax.ShapeDtypeStruct((KK, 1024, 256), BF16)
    return pl.pallas_call(
        forward_kernel,
        in_specs=[SMEM, HBM, HBM],
        out_specs=[VMEM] * 4,
        out_shape=[panel] * 2 + [half] * 2,
        scratch_shapes=[
            pltpu.VMEM((KK, 2, 32, 128), F32),
            pltpu.VMEM((KK, 2, 1024, 128), F32),
            pltpu.SemaphoreType.DMA((4,)),
            pltpu.SemaphoreType.DMA((16,)),
        ],
        compiler_params=params(24),
        cost_estimate=pl.CostEstimate(flops=3 * 2**30, bytes_accessed=21 * 2**20, transcendentals=0),
        name="forward_panel",
    )(pos, focusing, reflection)


def source_kernel(pos_ref, th_ref, tl_ref, tth_ref, ttl_ref, mute_ref, x_ref, time_ref, out_ref):
    turn = pos_ref[2]
    cols = []
    for j in range(2):
        groups = []
        for f in range(KB):
            t = [x_ref[place(f // 2, f % 2, i // 4, i % 4), j] for i in range(8)]
            groups.append(((t[0] + t[1]) + (t[2] + t[3])) + ((t[4] + t[5]) + (t[6] + t[7])))
        x = jnp.concatenate(groups, axis=0)
        cols.append(unturn(x.reshape(32, 8, 128), turn, -1).reshape(256, 128))
    up = mm3((th_ref[...], tl_ref[...]), split(jnp.concatenate(cols, axis=1)))
    t = lax.broadcasted_iota(jnp.int32, (NT, 128), 0)
    kept = []
    for j in range(2):
        mute = jnp.broadcast_to(mute_ref[j : j + 1, :], (NT, 128))
        val = jnp.where((t < mute) | (t > NT - mute), up[:, j * 128 : (j + 1) * 128], 0.0)
        time_ref[pl.ds(j, NT, stride=2), :] = val
        kept.append(val)
    back = mm3((tth_ref[...], ttl_ref[...]), split(jnp.concatenate(kept, axis=1)))
    for j in range(2):
        b = unturn(back[:, j * 128 : (j + 1) * 128].reshape(32, 8, 128), turn, 1)
        b = b.reshape(KB, 32, 128)
        for f in range(KB):
            for i in range(8):
                out_ref[place(f // 2, f % 2, i // 4, i % 4), j] = b[f]


def source_traces(pos, tables, mute, parts):
    return pl.pallas_call(
        source_kernel,
        in_specs=[SMEM] + [VMEM] * 6,
        out_specs=[VMEM] * 2,
        out_shape=[
            jax.ShapeDtypeStruct((NT * 2, 128), F32),
            jax.ShapeDtypeStruct((64, 2, 32, 128), F32),
        ],
        compiler_params=params(8),
        name="source_traces",
    )(pos, *tables, mute, parts)


def adjoint_kernel(second, own, oth, rh_ref, rl_ref, extra_ref, out_ref, time_hbm=None, sem=None):
    if not second:
        copy = pltpu.make_async_copy(extra_ref, time_hbm, sem)
        copy.start()
    pair = lax.broadcasted_iota(jnp.int32, (8, 128), 0) // 2
    even = (lax.broadcasted_iota(jnp.int32, (64, 128), 0) % 2) == 0

    for g in range(4):
        g8 = slice(g * 8, g * 8 + 8)
        acc = [None] * 4
        for zz in range(2):
            z = second * 2 + zz
            lhs = [[None] * 2 for _ in range(4)]
            for xh_ in range(2):
                tiles = [[] for _ in range(4)]
                for part in range(8):
                    j, xlo = part // 4, part % 2
                    if (part // 2) % 2:
                        v = [oth[place(zz, xh_, xlo, y), j, g8, :] for y in range(4)]
                    else:
                        v = [own[place(z, xh_, xlo, y), j, g8, :] for y in range(4)]
                    for q in range(4):
                        tiles[q].append(trade(v, pair, q))
                for q in range(4):
                    lhs[q][xh_] = jnp.concatenate(tiles[q], axis=0)
            rows = slice(z * 256, (z + 1) * 256)
            for q in range(4):
                bh, bl = split(jnp.concatenate(lhs[q], axis=1))
                wh, wl = rh_ref[g * 4 + q, rows, :], rl_ref[g * 4 + q, rows, :]
                both = mm(jnp.concatenate([bh, bl], axis=0), wh)
                add = both[:64] + (both[64:] + mm(bh, wl))
                acc[q] = add if acc[q] is None else acc[q] + add
        res = []
        for q in range(4):
            a, b = acc[q][:, :128], acc[q][:, 128:]
            res.append(a + jnp.where(even, pltpu.roll(b, 63, 0), -pltpu.roll(b, 1, 0)))
        for part in range(8):
            v = [r[part * 8 : part * 8 + 8] for r in res]
            for y in range(4):
                at = ((part % 2) * 4 + y, part // 2, g8, slice(None))
                t = trade(v, pair, y)
                out_ref[at] = extra_ref[at] + t if second else t
    if not second:
        copy.wait()


def adjoint_panel(second, own, oth, rh, rl, extra):
    panel = jax.ShapeDtypeStruct((8, 4, 32, 128), F32)
    time = jax.ShapeDtypeStruct((NT * 2, 128), F32)
    return pl.pallas_call(
        functools.partial(adjoint_kernel, second),
        in_specs=[VMEM] * 5,
        out_specs=VMEM if second else [VMEM, HBM],
        out_shape=panel if second else [panel, time],
        scratch_shapes=[] if second else [pltpu.SemaphoreType.DMA],
        compiler_params=params(8),
        cost_estimate=pl.CostEstimate(flops=3 * 2**29, bytes_accessed=2**20, transcendentals=0),
        name=f"adjoint_panel{second}",
    )(own, oth, rh, rl, extra)


def receiver_kernel(pos_ref, th_ref, tl_ref, mute_ref, direct_ref, x_ref, out_hbm, out_ref, sem):
    even = pos_ref[0] == 0
    turn = pos_ref[1]
    adj = []
    for c in range(2):
        cols = []
        for j in range(2):
            a = jnp.where(even, x_ref[:, j * 2 + c], x_ref[:, j * 2 + 1 - c])
            cols.append(unturn(a.reshape(32, 8, 128), turn, -1).reshape(256, 128))
        adj.append(mm3((th_ref[...], tl_ref[...]), split(jnp.concatenate(cols, axis=1))))
    copies = []
    for b in range(4):
        t = lax.broadcasted_iota(jnp.int32, (64, 128), 0) + b * 64
        for p in range(4):
            mute = jnp.broadcast_to(mute_ref[p : p + 1, :], (64, 128))
            val = adj[p // 2][b * 64 : b * 64 + 64, (p % 2) * 128 : (p % 2) * 128 + 128]
            rows = pl.ds(b * 256 + p, 64, stride=4)
            kept = jnp.where((t < mute) | (t > NT - mute), val, 0.0)
            out_ref[rows, :] = direct_ref[rows, :] - kept
        cut = pl.ds(b * 256, 256)
        copies.append(pltpu.make_async_copy(out_ref.at[cut], out_hbm.at[cut], sem.at[b]))
        copies[b].start()
    for copy in copies:
        copy.wait()


def receiver_traces(pos, tables, mute, direct, x):
    return pl.pallas_call(
        receiver_kernel,
        in_specs=[SMEM] + [VMEM] * 5,
        out_specs=HBM,
        out_shape=jax.ShapeDtypeStruct((NT * 4, 128), F32),
        scratch_shapes=[pltpu.VMEM((NT * 4, 128), F32), pltpu.SemaphoreType.DMA((4,))],
        compiler_params=params(8),
        name="receiver_traces",
    )(pos, *tables, mute, direct, x)


SWAP = [(0, 1), (1, 0)]
CHIPS = ("z", "xl", "xh", "y")


def exchange(x, axes):
    return lax.all_to_all(x, axes, split_axis=0, concat_axis=0, tiled=True)


def body(reflection, focusing, direct_wave, mute_source, mute_receiver):
    core, z, y = lax.axis_index("c"), lax.axis_index("z"), lax.axis_index("y")
    pos = jnp.stack([core, (z & 1) * 2 + lax.axis_index("xh"), y])
    table = dft_table()
    th, tl = split_const(table)

    focusing = pltpu.with_memory_space_constraint(focusing, pltpu.HBM)
    reflection = pltpu.with_memory_space_constraint(reflection, pltpu.HBM)
    own, oth, rh, rl = forward_panel(pos, focusing, reflection)
    parts = exchange(own + lax.ppermute(oth, "c", SWAP), CHIPS)
    time, back = source_traces(pos, (th, tl, th.T, tl.T), mute_source, parts)
    b_own = exchange(back, CHIPS)
    b_oth = [lax.ppermute(b_own[i * 32 : i * 32 + 32], "c", SWAP) for i in range(2)]
    adjoint, time = adjoint_panel(0, b_own, b_oth[0], rh, rl, time)
    adjoint = adjoint_panel(1, b_own, b_oth[1], rh, rl, adjoint)
    received = exchange(adjoint, ("z", "xh"))
    plus = receiver_traces(
        pos, (th, tl), mute_receiver, direct_wave.reshape(NT * 4, 128), received
    )
    return time.reshape(NT, 2, 128), plus.reshape(NT, 4, 128)


def solution(mesh):
    fine = Mesh(mesh.devices.reshape(4, 2, 2, 4, 2), ("z", "xh", "xl", "y", "c"))
    freq, rcv = ("z", "xh"), ("xl", "y", "c")
    return jax.shard_map(
        body,
        mesh=fine,
        in_specs=(
            P(freq, None, None, rcv),
            P(freq, None, None, rcv),
            P(None, freq, rcv),
            P(rcv, freq),
            P(freq, rcv),
        ),
        out_specs=(P(None, rcv, freq), P(None, freq, rcv)),
        check_vma=False,
    )
```
